32 devices in a mesh: tile: 8 (over y, x, core), grp: 4 (over z).
Axes of the slice: x: 2, y: 2, z: 4, core: 2. Of those that a mesh axis runs over, the one named last changes fastest.
Arguments:
- earlier_flow_speeds: float32 [2, 64, 256, 512], P(None, None, 'tile', 'grp'), may hold values from -6 to 6
- flow_rate_factor: float32 [64, 256, 512], P(None, 'tile', 'grp'), may hold values from 0.5 to 2
- scaled_warmth: float32 [64, 256, 512], P('grp', 'tile'), may hold values from -3 to 3
- gravity_forcing: float32 [2, 256, 512], P(None, 'tile', 'grp'), may hold values from -6 to 6
- sliding_coefficient: float32 [256, 512], P('tile', 'grp'), may hold values from 1 to 10
- icy_column_flag: int32 [256, 512], P('tile', 'grp'), may hold values 0 or 1
- resting_on_bed_flag: int32 [256, 512], P('tile', 'grp'), may hold values 0 or 1
Outputs:
- velocity: float32 [2, 64, 256, 512], P(None, None, 'tile', 'grp')
- temperature_next: float32 [64, 256, 512], P('grp', 'tile')
- hardness_next: float32 [64, 256, 512], P(None, 'tile', 'grp')
The draws below stay inside these ranges and needn't reach their ends.
All inputs are finite; a program needn't handle non-finite values. No bound on the sum of `icy_column_flag` or of `resting_on_bed_flag` on one device may be relied on, other than what follows from the above.
Results may differ from the reference program's by a relative error of at most 0.00002.
Values sent between devices are 32-bit elements; how exact they have to be, the bound alone decides.
A program may use at most 64 MiB of HBM per device.

```python
import math
import jax
import jax.numpy as jnp
from jax import lax

STRATA_NUMBER = 64
SWEEPS = 4
SECTIONS = 4
ZONAL_SPAN = 256
MERIDIONAL_SPAN = 512


def place_ends(array, own_key, low, largest):
    shape = array.shape
    place = [jax.random.randint(jax.random.fold_in(own_key, axis), (), 0, shape[axis]) for axis in range(len(shape))]
    array = array.at[tuple(place)].set(low)
    longest = shape.index(max(shape))
    place[longest] = (place[longest] + 1) % shape[longest]
    return array.at[tuple(place)].set(largest)


def block_scale(stream_key, extent, shards, smallest, largest):
    def one(dim, parts):
        steps = jax.random.uniform(jax.random.fold_in(jax.random.fold_in(stream_key, 6), dim), (parts,), jnp.float32, smallest / len(shards), largest / len(shards))
        return jnp.repeat(jnp.exp(steps), extent[dim] // parts).reshape((-1,) + (1,) * (len(extent) - dim - 1))

    factor_of = one(*shards[0])
    for cut in shards[1:]:
        factor_of = factor_of * one(*cut)
    return factor_of


def gaussian(stream_key, shape, scale, most, split=(), dtype=jnp.bfloat16):
    gain = block_scale(stream_key, shape, split, -0.22, 0.18) if split else 1.0
    entries = jax.random.normal(stream_key, shape, jnp.float32) * scale * gain
    return jnp.minimum(jnp.maximum(entries, -most), most).astype(dtype)


def setup_inputs(seed: int = 0) -> dict:
    arg_keys = jax.random.split(jax.random.key(seed), 8)
    earlier_flow_speeds = gaussian(arg_keys[0], (2, STRATA_NUMBER, ZONAL_SPAN, MERIDIONAL_SPAN), 1.0, 6.0, ((2, 8), (3, 4)), jnp.float32)
    flow_rate_factor = jnp.clip(jnp.exp(math.log(2.0) - 1.3862944 * jax.random.uniform(arg_keys[1], (STRATA_NUMBER, ZONAL_SPAN, MERIDIONAL_SPAN), jnp.float32) ** block_scale(arg_keys[1], (STRATA_NUMBER, ZONAL_SPAN, MERIDIONAL_SPAN), ((1, 8), (2, 4)), -0.2, 0.2)), 0.5, 2.0)
    scaled_warmth = gaussian(arg_keys[2], (STRATA_NUMBER, ZONAL_SPAN, MERIDIONAL_SPAN), 0.5, 3.0, ((0, 4), (1, 8)), jnp.float32)
    gravity_forcing = gaussian(arg_keys[3], (2, ZONAL_SPAN, MERIDIONAL_SPAN), 1.0, 6.0, ((1, 8), (2, 4)), jnp.float32)
    sliding_coefficient = jnp.clip(jnp.exp(math.log(10.0) - 2.3025851 * jax.random.uniform(arg_keys[4], (ZONAL_SPAN, MERIDIONAL_SPAN), jnp.float32) ** block_scale(arg_keys[4], (ZONAL_SPAN, MERIDIONAL_SPAN), ((0, 8), (1, 4)), -0.2, 0.2)), 1.0, 10.0)
    icy_column_flag = place_ends((jax.random.randint(arg_keys[5], (ZONAL_SPAN, MERIDIONAL_SPAN), 0, 4) < 3).astype(jnp.int32), jax.random.fold_in(arg_keys[5], 1), 0, 1)
    resting_on_bed_flag = place_ends((jax.random.randint(arg_keys[6], (ZONAL_SPAN, MERIDIONAL_SPAN), 0, 2) < 1).astype(jnp.int32), jax.random.fold_in(arg_keys[6], 1), 0, 1)
    return {"earlier_flow_speeds": earlier_flow_speeds, "flow_rate_factor": flow_rate_factor, "scaled_warmth": scaled_warmth, "gravity_forcing": gravity_forcing, "sliding_coefficient": sliding_coefficient, "icy_column_flag": icy_column_flag, "resting_on_bed_flag": resting_on_bed_flag}


vertical_weight = 4.0
strain_floor = 0.01
cross_weight = 0.75
diag_weight = 22.0
diffuse_flat = 0.1
diffuse_vert = 0.2
advect_weight = 0.05
heat_weight = 0.05
arrhenius = 0.6


def level_pad(field):
    return jnp.concatenate([field[:1], field, field[-1:]], axis=0)


def strain_parts(padded_u, padded_v):
    center_u = padded_u[:, 1:-1, 1:-1]
    center_v = padded_v[:, 1:-1, 1:-1]
    strain_xx = 0.5 * (padded_u[:, 2:, 1:-1] - padded_u[:, :-2, 1:-1])
    shear_uy = 0.5 * (padded_u[:, 1:-1, 2:] - padded_u[:, 1:-1, :-2])
    shear_vx = 0.5 * (padded_v[:, 2:, 1:-1] - padded_v[:, :-2, 1:-1])
    strain_yy = 0.5 * (padded_v[:, 1:-1, 2:] - padded_v[:, 1:-1, :-2])
    column_u = level_pad(center_u)
    column_v = level_pad(center_v)
    vert_u = 0.5 * (column_u[2:] - column_u[:-2])
    vert_v = 0.5 * (column_v[2:] - column_v[:-2])
    shear = shear_uy + shear_vx
    effective = (strain_xx * strain_xx + strain_yy * strain_yy + strain_xx * strain_yy
                 + 0.25 * shear * shear + 0.25 * (vert_u * vert_u + vert_v * vert_v))
    return effective, column_u, column_v


def viscosity_of(flow_rate_factor, effective):
    return flow_rate_factor * jnp.power(effective + strain_floor, -1.0 / 3.0)


def jacobi_sweep(padded_u, padded_v, flow_rate_factor, drive_u, driving_stress_north, drag_base, ice):
    effective, column_u, column_v = strain_parts(padded_u, padded_v)
    viscosity = viscosity_of(flow_rate_factor, effective)
    levels = padded_u.shape[0]
    bottom = (lax.broadcasted_iota(jnp.int32, (levels, 1, 1), 0) == 0).astype(jnp.float32)
    diagonal = viscosity * diag_weight + bottom * drag_base[None]
    near_u = (4.0 * (padded_u[:, 2:, 1:-1] + padded_u[:, :-2, 1:-1])
              + (padded_u[:, 1:-1, 2:] + padded_u[:, 1:-1, :-2])
              + vertical_weight * (column_u[2:] + column_u[:-2]))
    near_v = ((padded_v[:, 2:, 1:-1] + padded_v[:, :-2, 1:-1])
              + 4.0 * (padded_v[:, 1:-1, 2:] + padded_v[:, 1:-1, :-2])
              + vertical_weight * (column_v[2:] + column_v[:-2]))
    cross_u = cross_weight * (padded_v[:, 2:, 2:] - padded_v[:, :-2, 2:] - padded_v[:, 2:, :-2] + padded_v[:, :-2, :-2])
    cross_v = cross_weight * (padded_u[:, 2:, 2:] - padded_u[:, :-2, 2:] - padded_u[:, 2:, :-2] + padded_u[:, :-2, :-2])
    guard = diagonal + (1.0 - ice[None])
    new_u = ice[None] * (drive_u[None] + viscosity * (near_u + cross_u)) / guard
    new_v = ice[None] * (driving_stress_north[None] + viscosity * (near_v + cross_v)) / guard
    return jnp.stack([new_u, new_v])


def heating(padded_u, padded_v, flow_rate_factor, ice):
    effective, column_u, column_v = strain_parts(padded_u, padded_v)
    return ice[None] * 2.0 * viscosity_of(flow_rate_factor, effective) * effective


def thermal_section(padded, speed_u, speed_v, heat):
    center = padded[1:-1, 1:-1, 1:-1]
    east = padded[1:-1, 2:, 1:-1]
    west = padded[1:-1, :-2, 1:-1]
    north = padded[1:-1, 1:-1, 2:]
    south = padded[1:-1, 1:-1, :-2]
    upper = padded[2:, 1:-1, 1:-1]
    lower = padded[:-2, 1:-1, 1:-1]
    advect = (jnp.maximum(speed_u, 0.0) * (center - west) + jnp.minimum(speed_u, 0.0) * (east - center)
              + jnp.maximum(speed_v, 0.0) * (center - south) + jnp.minimum(speed_v, 0.0) * (north - center))
    return (center + diffuse_flat * (east + west + north + south - 4.0 * center)
            + diffuse_vert * (upper + lower - 2.0 * center) - advect_weight * advect + heat_weight * heat)


def reference(earlier_flow_speeds, flow_rate_factor, scaled_warmth, gravity_forcing, sliding_coefficient, icy_column_flag, resting_on_bed_flag):
    ice = icy_column_flag.astype(jnp.float32)
    drag_base = sliding_coefficient * resting_on_bed_flag.astype(jnp.float32)
    current = earlier_flow_speeds
    for sweep in range(SWEEPS):
        padded = jnp.pad(current, ((0, 0), (0, 0), (1, 1), (1, 1)))
        current = jacobi_sweep(padded[0], padded[1], flow_rate_factor, gravity_forcing[0], gravity_forcing[1], drag_base, ice)
    padded = jnp.pad(current, ((0, 0), (0, 0), (1, 1), (1, 1)))
    heat = heating(padded[0], padded[1], flow_rate_factor, ice)
    heat_content_field = scaled_warmth
    for section in range(SECTIONS):
        heat_content_field = thermal_section(jnp.pad(heat_content_field, 1), current[0], current[1], heat)
    return current, heat_content_field, jnp.exp(-arrhenius * heat_content_field)
```

```python
import functools

import jax
import jax.numpy as jnp
import numpy as np
from jax import lax
from jax.experimental import pallas as pl
from jax.experimental.pallas import tpu as pltpu
from jax.sharding import PartitionSpec as P

SWEEPS = 4
SECTIONS = 4
LANES = 128
SUB = 8
PAD = 8
UN = 4
PL = 2

MESH = pl.DeviceIdType.MESH
FOLD = 4.0 ** (1.0 / 3.0)
POWER = -1.0 / (3.0 * float(np.log(2.0)))


def roll(x, shift):
    return pltpu.roll(x, shift, 1)


def kernel(
    n,
    m,
    R,
    L,
    LG,
    segs_out,
    vel_in,
    rate_in,
    warm_in,
    grav,
    slide,
    icy,
    bed,
    vel_out,
    temp_out,
    hard_out,
    U0,
    U1,
    T0,
    T1,
    rate,
    coef,
    temp_st,
    hard_st,
    cb,
    pk,
    crx,
    mg,
    hx,
    tpk,
    trx,
    tmg,
    loc_sem,
    vs_sem,
    vr_sem,
    ts_sem,
    tr_sem,
    ws_sem,
    wr_sem,
    os_sem,
    or_sem,
    hs_sem,
):
    t = lax.axis_index("tile")
    g = lax.axis_index("grp")
    U = (U0, U1)
    T = (T0, T1)
    f32 = jnp.float32
    NS = R // SUB
    TOP = PAD + R
    Q = L // 4
    O, I = 0, 1
    SEGS = {O: ((0, Q), (L - Q, L)), I: ((Q, L - Q),)}

    def th_segs(k, G):
        if G == O:
            return ((0, Q - k), (L - Q + k, L))
        return ((Q - k, L - Q + k),)

    vel_cp = {
        G: [
            pltpu.make_async_copy(
                vel_in.at[:, a:b], U0.at[:, a:b, PAD:TOP, :], loc_sem.at[2 * G + i]
            )
            for i, (a, b) in enumerate(SEGS[G])
        ]
        for G in (O, I)
    }
    rate_cp = pltpu.make_async_copy(rate_in, rate, loc_sem.at[4])
    warm_cp = pltpu.make_async_copy(
        warm_in.at[:, :, pl.ds(pl.multiple_of(g * LANES, LANES), LANES)],
        T0.at[pl.ds(1 + g * LG, LG), PAD:TOP, :],
        loc_sem.at[5],
    )
    for G in (O, I):
        for cp in vel_cp[G]:
            cp.start()
    rate_cp.start()
    warm_cp.start()

    lo_t, hi_t, lo_g, hi_g = t > 0, t < n - 1, g > 0, g < m - 1

    def has(dt, dg):
        ok = None
        for d, lo, hi in ((dt, lo_t, hi_t), (dg, lo_g, hi_g)):
            if d:
                c = lo if d < 0 else hi
                ok = c if ok is None else jnp.logical_and(ok, c)
        return ok

    zero = jnp.zeros((SUB, LANES), f32)

    def clear_rows(l, c):
        for slot in range(2):
            for f in range(2):
                U[slot][f, l, 0:PAD, :] = zero
                U[slot][f, l, TOP : TOP + SUB, :] = zero
            T[slot][l + 1, 0:PAD, :] = zero
            T[slot][l + 1, TOP : TOP + SUB, :] = zero
        return c

    lax.fori_loop(0, L, clear_rows, 0)
    for slot in range(2):
        for l in (0, L + 1):
            T[slot][l] = jnp.zeros_like(T[slot][l])
    crx[...] = jnp.zeros_like(crx)
    trx[...] = jnp.zeros_like(trx)

    barrier = pltpu.get_barrier_semaphore()
    around = [(-1, -1), (-1, 0), (-1, 1), (1, -1), (1, 0), (1, 1)]
    for dt, dg in around:

        @pl.when(has(dt, dg))
        def _(dt=dt, dg=dg):
            pl.semaphore_signal(
                barrier, inc=1, device_id=(t + dt, g + dg), device_id_type=MESH
            )

    for d in range(1, m):
        pl.semaphore_signal(
            barrier, inc=1, device_id=(t, lax.rem(g + d, m)), device_id_type=MESH
        )

    sides_t = lo_t.astype(jnp.int32) + hi_t.astype(jnp.int32)
    sides_g = lo_g.astype(jnp.int32) + hi_g.astype(jnp.int32)
    pl.semaphore_wait(barrier, m - 1 + sides_t * (1 + sides_g))

    def vel_moves(k, G, part):
        slot = k % 2
        moves = []
        if part != "col":
            for a, b in SEGS[G]:
                if k == 0:
                    top, low = vel_in.at[:, a:b, R - 1, :], vel_in.at[:, a:b, 0, :]
                else:
                    top = U[slot].at[:, a:b, TOP - 1, :]
                    low = U[slot].at[:, a:b, PAD, :]
                moves += [
                    ((1, 0), top, U[slot].at[:, a:b, PAD - 1, :]),
                    ((-1, 0), low, U[slot].at[:, a:b, TOP, :]),
                ]
        if part != "row":
            moves += [
                ((0, 1), pk.at[k, G, PAD:TOP], crx.at[k, G, 0, PAD:TOP]),
                ((0, -1), pk.at[k, G, PAD:TOP], crx.at[k, G, 1, PAD:TOP]),
            ]
            if k < SWEEPS:
                for dg, side in ((1, 0), (-1, 1)):
                    moves += [
                        ((1, dg), pk.at[k, G, TOP - 1], crx.at[k, G, side, PAD - 1]),
                        ((-1, dg), pk.at[k, G, PAD], crx.at[k, G, side, TOP]),
                    ]
        first = 4 if part == "col" else 0
        if part == "all":
            rows = 2 * len(SEGS[G])
            index = list(range(rows)) + list(range(4, 4 + len(moves) - rows))
        else:
            index = list(range(first, first + len(moves)))
        return [
            (mv, vs_sem.at[k, G, j], vr_sem.at[k, G, j]) for mv, j in zip(moves, index)
        ]

    def th_moves(k, G):
        slot = k % 2
        moves = []
        for a, b in th_segs(k, G):
            moves += [
                ((1, 0), T[slot].at[1 + a : 1 + b, TOP - 1, :], T[slot].at[1 + a : 1 + b, PAD - 1, :]),
                ((-1, 0), T[slot].at[1 + a : 1 + b, PAD, :], T[slot].at[1 + a : 1 + b, TOP, :]),
            ]
        moves += [
            ((0, 1), tpk.at[k, G], trx.at[k, G, 0]),
            ((0, -1), tpk.at[k, G], trx.at[k, G, 1]),
        ]
        return [(mv, ts_sem.at[k, G, j], tr_sem.at[k, G, j]) for j, mv in enumerate(moves)]

    def remote(mv, s_sem, r_sem, sign=1):
        (dt, dg), src, dst = mv
        return pltpu.make_async_remote_copy(
            src,
            dst,
            s_sem,
            r_sem,
            device_id=(t + sign * dt, g + sign * dg),
            device_id_type=MESH,
        )

    def send(moves):
        for mv, s_sem, r_sem in moves:

            @pl.when(has(*mv[0]))
            def _(mv=mv, s_sem=s_sem, r_sem=r_sem):
                remote(mv, s_sem, r_sem).start()

    def sent(moves):
        for mv, s_sem, r_sem in moves:

            @pl.when(has(*mv[0]))
            def _(mv=mv, s_sem=s_sem, r_sem=r_sem):
                remote(mv, s_sem, r_sem).wait_send()

    def received(moves):
        for mv, s_sem, r_sem in moves:
            dt, dg = mv[0]

            @pl.when(has(-dt, -dg))
            def _(mv=mv, s_sem=s_sem, r_sem=r_sem):
                remote(mv, s_sem, r_sem, -1).wait_recv()

    up_half = 2 * g < m
    pieces = [(i, p) for i in range(m - 1) for p in range(LG // PL)]

    def target(i):
        asc = i + (i >= g).astype(jnp.int32)
        x = m - 1 - i
        desc = x - (x <= g).astype(jnp.int32)
        return jnp.where(up_half, desc, asc)

    def warm_piece(i, p):
        to = target(i)
        return pltpu.make_async_remote_copy(
            warm_in.at[
                p * PL : (p + 1) * PL, :, pl.ds(pl.multiple_of(to * LANES, LANES), LANES)
            ],
            T0.at[pl.ds(1 + g * LG + p * PL, PL), PAD:TOP, :],
            ws_sem.at[i, p],
            wr_sem.at[g, p],
            device_id=(t, to),
            device_id_type=MESH,
        )

    def warm_recv(src, p):
        part = T0.at[1 + src * LG + p * PL : 1 + src * LG + (p + 1) * PL, PAD:TOP, :]
        return pltpu.make_async_remote_copy(
            part, part, ws_sem.at[0, p], wr_sem.at[src, p], device_id=(t, g), device_id_type=MESH
        )

    outer = jnp.logical_or(g * LG < Q, (g + 1) * LG > L - Q)
    SLOTS = 10
    OUTER_SLOTS = {s: (s * 3, s * 3 + 3) for s in range(8)}
    INNER_SLOTS = {4: (0, 4), 5: (4, 8), 6: (8, 12), 7: (12, 18), 8: (18, 24)}

    def bulk(slot):
        for cond, table in ((outer, OUTER_SLOTS), (jnp.logical_not(outer), INNER_SLOTS)):
            if slot in table:
                a, b = table[slot]

                @pl.when(cond)
                def _(a=a, b=b):
                    for i, p in pieces[a:b]:
                        warm_piece(i, p).start()

    def warm_arrived(sources):
        for src in sources:

            @pl.when(g == src)
            def _():
                warm_cp.wait()

            @pl.when(g != src)
            def _(src=src):
                for p in range(LG // PL):
                    warm_recv(src, p).wait_recv()

    lane = lax.broadcasted_iota(jnp.int32, (SUB, LANES), 1)
    first = lane == 0
    last = lane == LANES - 1
    odd = lax.rem(lane, 2) == 1
    pair = lax.div(lane, 2)

    def sides(x, edge):
        up = jnp.where(last, edge, roll(x, LANES - 1))
        down = jnp.where(first, edge, roll(x, 1))
        return up, down

    def rows(s, d=0):
        return slice(PAD + s * SUB + d, PAD + s * SUB + d + SUB)

    def tile(s):
        return slice(s * SUB, (s + 1) * SUB)

    def base(G, a):
        return a if G == O and a < Q else (a - L // 2 if G == O else a - Q)

    def levels(a, b, body):
        steps = -(-(b - a) // UN)

        def step(i, c):
            body(jnp.minimum(a + i * UN, b - UN))
            return c

        lax.fori_loop(0, steps, step, 0)

    def spots(j):
        pu = 2 * j
        return (
            (pair == j, pu + 1, lax.rem(2 * LANES - 2 - pu, LANES)),
            (
                pair == j + LANES // 4,
                lax.rem(pu + LANES // 2 + 1, LANES),
                lax.rem(2 * LANES - 2 - LANES // 2 - pu, LANES),
            ),
        )

    def put_pack(k, G, s, sp, new):
        acc = pk[k, G, rows(s), :]
        for (hit, to, _), x in zip(sp, new):
            acc = jnp.where(hit, roll(x, to), acc)
        pk[k, G, rows(s), :] = acc

    def pack_first(G):
        for a, b in SEGS[G]:
            off = a - base(G, a)

            def body(l0, off=off):
                for j in range(UN):
                    l = l0 + j
                    sp = spots(l - off)
                    for s in range(NS):
                        put_pack(0, G, s, sp, [U0[f, l, rows(s), :] for f in range(2)])

            levels(a, b, body)

    def merge(k, G):
        for s in range(-1, NS + 1):
            w = jnp.where(odd, crx[k, G, 1, rows(s), :], roll(crx[k, G, 0, rows(s), :], 2))
            mg[G, rows(s), :] = w
        if k < SWEEPS:
            for s in range(NS):
                hx[G, tile(s), :] = mg[G, rows(s, 1), :] - mg[G, rows(s, -1), :]

    def strain(slot, G, l, s, sp):
        lm = jnp.maximum(l - 1, 0)
        lp = jnp.minimum(l + 1, L - 1)
        V = U[slot]
        halo = mg[G, rows(s), :]
        c, e, w, up, lo = [], [], [], [], []
        for f in range(2):
            c.append(V[f, l, rows(s), :])
            e.append(V[f, l, rows(s, 1), :])
            w.append(V[f, l, rows(s, -1), :])
            up.append(V[f, lp, rows(s), :])
            lo.append(V[f, lm, rows(s), :])
        nn, ss = zip(*[sides(c[f], roll(halo, sp[f][2])) for f in range(2)])
        xu, xv = e[0] - w[0], e[1] - w[1]
        yv = nn[1] - ss[1]
        shear = (nn[0] - ss[0]) + xv
        du, dv = up[0] - lo[0], up[1] - lo[1]
        total = (xu * (xu + yv) + yv * yv) + 0.25 * (
            (shear * shear + du * du) + dv * dv
        )
        visc = rate[l, tile(s), :] * jnp.exp2(jnp.log(total + 0.04) * POWER)
        return c, e, w, up, lo, nn, ss, xu, xv, total, visc

    def sweep(k, G):
        slot, new_slot = k % 2, (k + 1) % 2
        for a, b in SEGS[G]:
            off = a - base(G, a)

            def body(l0, off=off):
                for j in range(UN):
                    l = l0 + j
                    sp = spots(l - off)
                    for s in range(NS):
                        _, e, w, up, lo, nn, ss, xu, xv, _, visc = strain(slot, G, l, s, sp)
                        hxv = hx[G, tile(s), :]
                        nu, su = sides(xu, roll(hxv, sp[0][2]))
                        nv, sv = sides(xv, roll(hxv, sp[1][2]))
                        near_u = (
                            4.0 * ((e[0] + w[0]) + (up[0] + lo[0]))
                            + (nn[0] + ss[0])
                            + 0.75 * (nv - sv)
                        )
                        near_v = (
                            4.0 * ((nn[1] + ss[1]) + (up[1] + lo[1]))
                            + (e[1] + w[1])
                            + 0.75 * (nu - su)
                        )
                        diagonal = 22.0 * visc + cb[3 + jnp.minimum(l, 1), tile(s), :]
                        scale = cb[0, tile(s), :] / diagonal
                        new = (
                            (cb[1, tile(s), :] + visc * near_u) * scale,
                            (cb[2, tile(s), :] + visc * near_v) * scale,
                        )
                        for f in range(2):
                            U[new_slot][f, l, rows(s), :] = new[f]
                        put_pack(k + 1, G, s, sp, new)

            levels(a, b, body)

    def heat(G):
        slot = SWEEPS % 2
        for a, b in SEGS[G]:
            off = a - base(G, a)

            def body(l0, off=off):
                for j in range(UN):
                    l = l0 + j
                    sp = spots(l - off)
                    for s in range(NS):
                        c, *_, total, visc = strain(slot, G, l, s, sp)
                        q = (cb[0, tile(s), :] * (0.025 * FOLD)) * (visc * total)
                        u, v = 0.05 * c[0], 0.05 * c[1]
                        west = 0.1 + jnp.maximum(u, 0.0)
                        east = 0.1 - jnp.minimum(u, 0.0)
                        south = 0.1 + jnp.maximum(v, 0.0)
                        north = 0.1 - jnp.minimum(v, 0.0)
                        mid = 0.6 - ((west + east) + (south + north))
                        for i, x in enumerate((q, west, east, south, north, mid)):
                            coef[i, l, tile(s), :] = x

            levels(a, b, body)

    def put_tpack(k, G, l, s, x):
        tpk[k, G, tile(s), :] = jnp.where(
            pair == l, roll(x, 2 * l + 1), tpk[k, G, tile(s), :]
        )

    def theta_first(G):
        for a, b in th_segs(0, G):

            def body(l0):
                for j in range(UN):
                    l = l0 + j
                    for s in range(NS):
                        put_tpack(0, G, l, s, T0[l + 1, rows(s), :])

            levels(a, b, body)

    def th_merge(k, G):
        for s in range(NS):
            w = jnp.where(odd, trx[k, G, 1, tile(s), :], roll(trx[k, G, 0, tile(s), :], 2))
            if G == I:
                (a, b), = th_segs(k, I)
                mine = jnp.logical_and(lane > 2 * a, lane <= 2 * b)
                w = jnp.where(mine, w, tmg[k, tile(s), :])
            tmg[k, tile(s), :] = w

    def section(k, G):
        slot, new_slot = k % 2, (k + 1) % 2
        for a, b in th_segs(k + 1, G):

            def body(l0):
                for j in range(UN):
                    l = l0 + j
                    for s in range(NS):
                        V = T[slot]
                        c = V[l + 1, rows(s), :]
                        nn, ss = sides(c, roll(tmg[k, tile(s), :], 2 * LANES - 2 - 2 * l - LANES))
                        q, west, east, south, north, mid = [
                            coef[i, l, tile(s), :] for i in range(6)
                        ]
                        value = (
                            (mid * c + 0.2 * (V[l + 2, rows(s), :] + V[l, rows(s), :]))
                            + (west * V[l + 1, rows(s, -1), :] + east * V[l + 1, rows(s, 1), :])
                            + ((south * ss + north * nn) + q)
                        )
                        if k < SECTIONS - 1:
                            T[new_slot][l + 1, rows(s), :] = value
                            put_tpack(k + 1, G, l, s, value)
                        else:
                            temp_st[l, tile(s), :] = value
                            hard_st[l, tile(s), :] = jnp.exp(-0.6 * value)

            levels(a, b, body)

    def temp_move(i):
        q, a, b = segs_out[i][1:]
        src = temp_st.at[a:b]
        dst = temp_out.at[
            a - q * LG : b - q * LG, :, pl.ds(pl.multiple_of(g * LANES, LANES), LANES)
        ]
        far = pltpu.make_async_remote_copy(
            src, dst, os_sem.at[i], or_sem.at[i, g], device_id=(t, q), device_id_type=MESH
        )
        return far, pltpu.make_async_copy(src, dst, os_sem.at[i])

    def temp_send(i):
        q = segs_out[i][1]

        @pl.when(g != q)
        def _():
            temp_move(i)[0].start()

        @pl.when(g == q)
        def _():
            temp_move(i)[1].start()

    def temp_wait(i):
        q, a, b = segs_out[i][1:]

        @pl.when(g != q)
        def _():
            temp_move(i)[0].wait_send()

        @pl.when(g == q)
        def _():
            temp_move(i)[1].wait()
            for src in range(m):
                if src != q:
                    dst = temp_out.at[
                        a - q * LG : b - q * LG, :, src * LANES : (src + 1) * LANES
                    ]
                    pltpu.make_async_remote_copy(
                        dst, dst, os_sem.at[i], or_sem.at[i, src],
                        device_id=(t, g), device_id_type=MESH,
                    ).wait_recv()

    for G in (O, I):
        send(vel_moves(0, G, "row"))
    bulk(0)
    for G in (O, I):
        for cp in vel_cp[G]:
            cp.wait()
        pack_first(G)
        send(vel_moves(0, G, "col"))
    bulk(1)
    ice = icy[...].astype(f32)
    water = (1.0 - ice) * (1.0 / FOLD)
    cb[0] = ice
    cb[1] = grav[0] * (1.0 / FOLD)
    cb[2] = grav[1] * (1.0 / FOLD)
    cb[3] = water + slide[...] * bed[...].astype(f32) * (1.0 / FOLD)
    cb[4] = water
    rate_cp.wait()

    vel_back = {
        G: [
            pltpu.make_async_copy(
                U[SWEEPS % 2].at[:, a:b, PAD:TOP, :], vel_out.at[:, a:b], hs_sem.at[2 * G + i]
            )
            for i, (a, b) in enumerate(SEGS[G])
        ]
        for G in (O, I)
    }
    for k in range(SWEEPS):
        for G in (O, I):
            received(vel_moves(k, G, "all"))
            if k:
                sent(vel_moves(k - 1, G, "all"))
            merge(k, G)
            sweep(k, G)
            send(vel_moves(k + 1, G, "all"))
            bulk(2 + 2 * k + G)
            if k == SWEEPS - 1:
                for cp in vel_back[G]:
                    cp.start()

    def owners(G):
        return sorted({q for q in range(m) for a, b in th_segs(0, G) if a < (q + 1) * LG and b > q * LG})

    def heat_part(G):
        received(vel_moves(SWEEPS, G, "all"))
        merge(SWEEPS, G)
        heat(G)

    def th_part(k, G):
        received(th_moves(k, G))
        th_merge(k, G)
        if k:
            sent(th_moves(k - 1, G))
        section(k, G)
        if k < SECTIONS - 1:
            send(th_moves(k + 1, G))
        else:
            for i, sg in enumerate(segs_out):
                if sg[0] == G:
                    temp_send(i)
            for cp in hard_back[G]:
                cp.start()

    def th_start(G, known=()):
        warm_arrived([q for q in owners(G) if q not in known])
        theta_first(G)
        send(th_moves(0, G))

    hard_back = {
        G: [
            pltpu.make_async_copy(hard_st.at[a:b], hard_out.at[a:b], hs_sem.at[4 + 2 * G + i])
            for i, (a, b) in enumerate(th_segs(SECTIONS, G))
        ]
        for G in (O, I)
    }
    th_start(O)
    heat_part(O)
    th_part(0, O)
    heat_part(I)
    th_start(I, owners(O))
    th_part(1, O)
    th_part(0, I)
    th_part(2, O)
    th_part(1, I)
    th_part(3, O)
    th_part(2, I)
    th_part(3, I)

    for i in range(len(segs_out)):
        temp_wait(i)
    for i, p in pieces:
        warm_piece(i, p).wait_send()
    for G in (O, I):
        for cp in vel_back[G] + hard_back[G]:
            cp.wait()
        sent(vel_moves(SWEEPS - 1, G, "all"))
        sent(vel_moves(SWEEPS, G, "all"))
        sent(th_moves(SECTIONS - 1, G))


def local(n, m, vel, rate, warm, grav, slide, icy, bed):
    _, L, R, Y = vel.shape
    LG = L // m
    assert Y == LANES and R % SUB == 0 and L % (4 * UN) == 0 and LG % PL == 0
    assert 2 * L == LANES and L // 4 > SECTIONS + UN
    f32 = jnp.float32
    Q = L // 4
    cut = SECTIONS
    parts = [(0, 0, Q - cut), (0, L - Q + cut, L), (1, Q - cut, L - Q + cut)]
    segs_out = []
    for G, a, b in parts:
        while a < b:
            q = a // LG
            e = min(b, (q + 1) * LG)
            segs_out.append((G, q, a, e))
            a = e
    segs_out = tuple(segs_out)
    any_spec = pl.BlockSpec(memory_space=pl.ANY)
    vmem = pl.BlockSpec(memory_space=pltpu.VMEM)
    K = SWEEPS + 1
    H = R + 2 * PAD
    V = pltpu.VMEM
    dma = pltpu.SemaphoreType.DMA
    return pl.pallas_call(
        functools.partial(kernel, n, m, R, L, LG, segs_out),
        out_shape=(
            jax.ShapeDtypeStruct(vel.shape, f32),
            jax.ShapeDtypeStruct(warm.shape, f32),
            jax.ShapeDtypeStruct(rate.shape, f32),
        ),
        in_specs=[any_spec] * 3 + [vmem] * 4,
        out_specs=(any_spec,) * 3,
        scratch_shapes=[
            V((2, L, H, LANES), f32),
            V((2, L, H, LANES), f32),
            V((L + 2, H, LANES), f32),
            V((L + 2, H, LANES), f32),
            V((L, R, LANES), f32),
            V((6, L, R, LANES), f32),
            V((L, R, LANES), f32),
            V((L, R, LANES), f32),
            V((5, R, LANES), f32),
            V((K, 2, H, LANES), f32),
            V((K, 2, 2, H, LANES), f32),
            V((2, H, LANES), f32),
            V((2, R, LANES), f32),
            V((SECTIONS, 2, R, LANES), f32),
            V((SECTIONS, 2, 2, R, LANES), f32),
            V((SECTIONS, R, LANES), f32),
            dma((6,)),
            dma((K, 2, 10)),
            dma((K, 2, 10)),
            dma((SECTIONS, 2, 6)),
            dma((SECTIONS, 2, 6)),
            dma((m - 1, LG // PL)),
            dma((m, LG // PL)),
            dma((len(segs_out),)),
            dma((len(segs_out), m)),
            dma((8,)),
        ],
        compiler_params=pltpu.CompilerParams(
            collective_id=0, has_side_effects=True, vmem_limit_bytes=60 * 1024 * 1024
        ),
        name="ice_step",
    )(vel, rate, warm, grav, slide, icy, bed)


def solution(mesh):
    return jax.shard_map(
        functools.partial(local, mesh.shape["tile"], mesh.shape["grp"]),
        mesh=mesh,
        in_specs=(
            P(None, None, "tile", "grp"),
            P(None, "tile", "grp"),
            P("grp", "tile", None),
            P(None, "tile", "grp"),
            P("tile", "grp"),
            P("tile", "grp"),
            P("tile", "grp"),
        ),
        out_specs=(P(None, None, "tile", "grp"), P("grp", "tile", None), P(None, "tile", "grp")),
        check_vma=False,
    )
```

```python
import functools

import jax
import jax.numpy as jnp
from jax import lax
from jax.experimental import pallas as pl
from jax.experimental.pallas import tpu as pltpu
from jax.sharding import PartitionSpec as P

SWEEPS = 4
SECTIONS = 4
LANES = 128
SUB = 8
PAD = 8
UB = 2
UT = 4
PL = 2

MESH = pl.DeviceIdType.MESH
FOLD = 4.0 ** (1.0 / 3.0)


def roll(x, shift):
    return pltpu.roll(x, shift, 1)


def kernel(
    n,
    m,
    R,
    L,
    LG,
    segs_out,
    vel_in,
    rate_in,
    warm_in,
    grav,
    slide,
    icy,
    bed,
    vel_out,
    temp_out,
    hard_out,
    U0,
    U1,
    T0,
    T1,
    rate,
    coef,
    temp_st,
    hard_st,
    cb,
    dya,
    dyb,
    sya,
    syb,
    nsa,
    nsb,
    pk,
    crx,
    mg,
    tpk,
    trx,
    tmg,
    loc_sem,
    vs_sem,
    vr_sem,
    ts_sem,
    tr_sem,
    ws_sem,
    wr_sem,
    os_sem,
    or_sem,
    hs_sem,
):
    t = lax.axis_index("tile")
    g = lax.axis_index("grp")
    U = (U0, U1)
    T = (T0, T1)
    f32 = jnp.float32
    NS = R // SUB
    TOP = PAD + R
    Q = L // 4
    O, I = 0, 1
    SEGS = {O: ((0, Q), (L - Q, L)), I: ((Q, L - Q),)}

    def th_segs(k, G):
        if G == O:
            return ((0, Q - k), (L - Q + k, L))
        return ((Q - k, L - Q + k),)

    vel_cp = {
        G: [
            pltpu.make_async_copy(
                vel_in.at[:, a:b], U0.at[:, a:b, PAD:TOP, :], loc_sem.at[2 * G + i]
            )
            for i, (a, b) in enumerate(SEGS[G])
        ]
        for G in (O, I)
    }
    rate_cp = pltpu.make_async_copy(rate_in, rate, loc_sem.at[4])
    warm_cp = pltpu.make_async_copy(
        warm_in.at[:, :, pl.ds(pl.multiple_of(g * LANES, LANES), LANES)],
        T0.at[pl.ds(1 + g * LG, LG), PAD:TOP, :],
        loc_sem.at[5],
    )
    for G in (O, I):
        for cp in vel_cp[G]:
            cp.start()
    rate_cp.start()
    warm_cp.start()

    lo_t, hi_t, lo_g, hi_g = t > 0, t < n - 1, g > 0, g < m - 1

    def has(dt, dg):
        ok = None
        for d, lo, hi in ((dt, lo_t, hi_t), (dg, lo_g, hi_g)):
            if d:
                c = lo if d < 0 else hi
                ok = c if ok is None else jnp.logical_and(ok, c)
        return ok

    zero = jnp.zeros((SUB, LANES), f32)

    def clear_rows(l, c):
        for slot in range(2):
            for f in range(2):
                U[slot][f, l, 0:PAD, :] = zero
                U[slot][f, l, TOP : TOP + SUB, :] = zero
            T[slot][l + 1, 0:PAD, :] = zero
            T[slot][l + 1, TOP : TOP + SUB, :] = zero
        return c

    lax.fori_loop(0, L, clear_rows, 0)
    for slot in range(2):
        for l in (0, L + 1):
            T[slot][l] = jnp.zeros_like(T[slot][l])
    crx[...] = jnp.zeros_like(crx)
    trx[...] = jnp.zeros_like(trx)

    barrier = pltpu.get_barrier_semaphore()
    around = [(-1, -1), (-1, 0), (-1, 1), (1, -1), (1, 0), (1, 1)]
    for dt, dg in around:

        @pl.when(has(dt, dg))
        def _(dt=dt, dg=dg):
            pl.semaphore_signal(
                barrier, inc=1, device_id=(t + dt, g + dg), device_id_type=MESH
            )

    for d in range(1, m):
        pl.semaphore_signal(
            barrier, inc=1, device_id=(t, lax.rem(g + d, m)), device_id_type=MESH
        )

    sides_t = lo_t.astype(jnp.int32) + hi_t.astype(jnp.int32)
    sides_g = lo_g.astype(jnp.int32) + hi_g.astype(jnp.int32)
    pl.semaphore_wait(barrier, m - 1 + sides_t * (1 + sides_g))

    def vel_moves(k, G, part):
        slot = k % 2
        moves = []
        if part != "col":
            for a, b in SEGS[G]:
                if k == 0:
                    top, low = vel_in.at[:, a:b, R - 1, :], vel_in.at[:, a:b, 0, :]
                else:
                    top = U[slot].at[:, a:b, TOP - 1, :]
                    low = U[slot].at[:, a:b, PAD, :]
                moves += [
                    ((1, 0), top, U[slot].at[:, a:b, PAD - 1, :]),
                    ((-1, 0), low, U[slot].at[:, a:b, TOP, :]),
                ]
        if part != "row":
            moves += [
                ((0, 1), pk.at[k, G, PAD:TOP], crx.at[k, G, 0, PAD:TOP]),
                ((0, -1), pk.at[k, G, PAD:TOP], crx.at[k, G, 1, PAD:TOP]),
            ]
            if k < SWEEPS:
                for dg, side in ((1, 0), (-1, 1)):
                    moves += [
                        ((1, dg), pk.at[k, G, TOP - 1], crx.at[k, G, side, PAD - 1]),
                        ((-1, dg), pk.at[k, G, PAD], crx.at[k, G, side, TOP]),
                    ]
        first = 4 if part == "col" else 0
        if part == "all":
            rows = 2 * len(SEGS[G])
            index = list(range(rows)) + list(range(4, 4 + len(moves) - rows))
        else:
            index = list(range(first, first + len(moves)))
        return [
            (mv, vs_sem.at[k, G, j], vr_sem.at[k, G, j]) for mv, j in zip(moves, index)
        ]

    def th_moves(k, G):
        slot = k % 2
        moves = []
        for a, b in th_segs(k, G):
            moves += [
                ((1, 0), T[slot].at[1 + a : 1 + b, TOP - 1, :], T[slot].at[1 + a : 1 + b, PAD - 1, :]),
                ((-1, 0), T[slot].at[1 + a : 1 + b, PAD, :], T[slot].at[1 + a : 1 + b, TOP, :]),
            ]
        moves += [
            ((0, 1), tpk.at[k, G], trx.at[k, G, 0]),
            ((0, -1), tpk.at[k, G], trx.at[k, G, 1]),
        ]
        return [(mv, ts_sem.at[k, G, j], tr_sem.at[k, G, j]) for j, mv in enumerate(moves)]

    def remote(mv, s_sem, r_sem, sign=1):
        (dt, dg), src, dst = mv
        return pltpu.make_async_remote_copy(
            src,
            dst,
            s_sem,
            r_sem,
            device_id=(t + sign * dt, g + sign * dg),
            device_id_type=MESH,
        )

    def send(moves):
        for mv, s_sem, r_sem in moves:

            @pl.when(has(*mv[0]))
            def _(mv=mv, s_sem=s_sem, r_sem=r_sem):
                remote(mv, s_sem, r_sem).start()

    def sent(moves):
        for mv, s_sem, r_sem in moves:

            @pl.when(has(*mv[0]))
            def _(mv=mv, s_sem=s_sem, r_sem=r_sem):
                remote(mv, s_sem, r_sem).wait_send()

    def received(moves):
        for mv, s_sem, r_sem in moves:
            dt, dg = mv[0]

            @pl.when(has(-dt, -dg))
            def _(mv=mv, s_sem=s_sem, r_sem=r_sem):
                remote(mv, s_sem, r_sem, -1).wait_recv()

    up_half = 2 * g < m
    pieces = [(i, p) for i in range(m - 1) for p in range(LG // PL)]

    def target(i):
        asc = i + (i >= g).astype(jnp.int32)
        x = m - 1 - i
        desc = x - (x <= g).astype(jnp.int32)
        return jnp.where(up_half, desc, asc)

    def warm_piece(i, p):
        to = target(i)
        return pltpu.make_async_remote_copy(
            warm_in.at[
                p * PL : (p + 1) * PL, :, pl.ds(pl.multiple_of(to * LANES, LANES), LANES)
            ],
            T0.at[pl.ds(1 + g * LG + p * PL, PL), PAD:TOP, :],
            ws_sem,
            wr_sem.at[g],
            device_id=(t, to),
            device_id_type=MESH,
        )

    def warm_recv(src):
        part = T0.at[1 + src * LG : 1 + (src + 1) * LG, PAD:TOP, :]
        return pltpu.make_async_remote_copy(
            part, part, ws_sem, wr_sem.at[src], device_id=(t, g), device_id_type=MESH
        )

    def warm_sent():
        part = temp_st.at[0 : (m - 1) * LG]
        pltpu.make_async_remote_copy(
            part, part, ws_sem, wr_sem.at[0], device_id=(t, g), device_id_type=MESH
        ).wait_send()

    outer = jnp.logical_or(g * LG < Q, (g + 1) * LG > L - Q)
    SLOTS = 10
    OUTER_SLOTS = {s: (s * 3, s * 3 + 3) for s in range(8)}
    INNER_SLOTS = {4: (0, 4), 5: (4, 8), 6: (8, 12), 7: (12, 18), 8: (18, 24)}

    def bulk(slot):
        for cond, table in ((outer, OUTER_SLOTS), (jnp.logical_not(outer), INNER_SLOTS)):
            if slot in table:
                a, b = table[slot]

                @pl.when(cond)
                def _(a=a, b=b):
                    for i, p in pieces[a:b]:
                        warm_piece(i, p).start()

    def warm_arrived(sources):
        for src in sources:

            @pl.when(g == src)
            def _():
                warm_cp.wait()

            @pl.when(g != src)
            def _(src=src):
                warm_recv(src).wait_recv()

    lane = lax.broadcasted_iota(jnp.int32, (SUB, LANES), 1)
    first = lane == 0
    last = lane == LANES - 1
    odd = lax.rem(lane, 2) == 1
    pair = lax.div(lane, 2)
    bottom = lax.broadcasted_iota(jnp.int32, (SUB, LANES), 0) == SUB - 1

    def rows(s, d=0):
        return slice(PAD + s * SUB + d, PAD + s * SUB + d + SUB)

    def tile(s):
        return slice(s * SUB, (s + 1) * SUB)

    HB = L // 2 // (2 * UB)

    def start_of(G, i):
        i = jnp.minimum(i, HB - 1) * (2 * UB)
        if G == I:
            return i + Q, i
        return i + jnp.where(i >= Q, L // 2, 0), i

    def edge_spot(j):
        return (
            lax.rem(2 * LANES - 2 - 2 * j, LANES),
            lax.rem(2 * LANES - 2 - LANES // 2 - 2 * j, LANES),
        )

    def pack_spot(j):
        return (
            (pair == j, 2 * j + 1),
            (pair == j + LANES // 4, lax.rem(2 * j + LANES // 2 + 1, LANES)),
        )

    def pack_vel(k, G, l, j):
        for d in range(UB):
            sp = pack_spot(j + d)
            for s in range(NS):
                for f in range(2):
                    hit, to = sp[f]
                    pltpu.store(
                        pk.at[k, G, rows(s), :],
                        roll(U[k % 2][f, l + d, rows(s), :], to),
                        mask=hit,
                    )

    def pack_first(G):
        def body(i, c):
            l, j = start_of(G, i)
            pack_vel(0, G, l, j)
            pack_vel(0, G, l + UB, j + UB)
            return c

        lax.fori_loop(0, HB, body, 0)

    def merge(k, G):
        for s in range(-1, NS + 1):
            w = jnp.where(odd, crx[k, G, 1, rows(s), :], roll(crx[k, G, 0, rows(s), :], 2))
            mg[G, rows(s), :] = w
            if s == -1:
                low = w
        mg[G, rows(NS), :] = jnp.where(bottom, low, w)

    def side_vel(k, G, l, j, dy, sy):
        V = U[k % 2]
        tiles = NS + 1 if k < SWEEPS else NS
        for d in range(UB):
            sp = edge_spot(j + d)
            for s in range(tiles):
                halo = mg[G, rows(s), :]
                for f in range(2):
                    x = V[f, l + d, rows(s), :]
                    if s == NS:
                        x = jnp.where(bottom, V[f, l + d, rows(-1), :], x)
                    edge = roll(halo, sp[f])
                    up = jnp.where(last, edge, roll(x, LANES - 1))
                    down = jnp.where(first, edge, roll(x, 1))
                    diff = up - down
                    dy[f, d, rows(s), :] = diff
                    if s == NS:
                        dy[f, d, rows(-1), :] = diff
                    elif k < SWEEPS:
                        sy[f, d, tile(s), :] = up + down

    def strain(slot, l, d, s, dy):
        l = l + d
        lm = jnp.maximum(l - 1, 0)
        lp = jnp.minimum(l + 1, L - 1)
        V = U[slot]
        e, w, up, lo = [], [], [], []
        for f in range(2):
            e.append(V[f, l, rows(s, 1), :])
            w.append(V[f, l, rows(s, -1), :])
            up.append(V[f, lp, rows(s), :])
            lo.append(V[f, lm, rows(s), :])
        xu, xv = e[0] - w[0], e[1] - w[1]
        yv = dy[1, d, rows(s), :]
        shear = dy[0, d, rows(s), :] + xv
        du, dv = up[0] - lo[0], up[1] - lo[1]
        total = (xu * (xu + yv) + yv * yv) + 0.25 * (
            (shear * shear + du * du) + dv * dv
        )
        visc = rate[l, tile(s), :] * jnp.exp2(lax.log2(total + 0.04) * (-1.0 / 3.0))
        return e, w, up, lo, total, visc

    def new_vel(k, l, dy, sy):
        slot, new_slot = k % 2, (k + 1) % 2
        for d in range(UB):
            low = jnp.minimum(l + d, 1)
            for s in range(NS):
                e, w, up, lo, _, visc = strain(slot, l, d, s, dy)
                cross_u = dy[1, d, rows(s, 1), :] - dy[1, d, rows(s, -1), :]
                cross_v = dy[0, d, rows(s, 1), :] - dy[0, d, rows(s, -1), :]
                near_u = (
                    4.0 * ((e[0] + w[0]) + (up[0] + lo[0]))
                    + sy[0, d, tile(s), :]
                    + 0.75 * cross_u
                )
                near_v = (
                    4.0 * (sy[1, d, tile(s), :] + (up[1] + lo[1]))
                    + (e[1] + w[1])
                    + 0.75 * cross_v
                )
                scale = 1.0 / (22.0 * visc + cb[2 + low, tile(s), :])
                U[new_slot][0, l + d, rows(s), :] = (cb[0, tile(s), :] + visc * near_u) * scale
                U[new_slot][1, l + d, rows(s), :] = (cb[1, tile(s), :] + visc * near_v) * scale

    def new_heat(l, dy):
        slot = SWEEPS % 2
        for d in range(UB):
            for s in range(NS):
                *_, total, visc = strain(slot, l, d, s, dy)
                q = (0.025 * FOLD) * (visc * total)
                u = 0.05 * U[slot][0, l + d, rows(s), :]
                v = 0.05 * U[slot][1, l + d, rows(s), :]
                west = 0.1 + jnp.maximum(u, 0.0)
                east = 0.1 - jnp.minimum(u, 0.0)
                south = 0.1 + jnp.maximum(v, 0.0)
                north = 0.1 - jnp.minimum(v, 0.0)
                mid = 0.6 - ((west + east) + (south + north))
                for i, x in enumerate((q, west, east, south, north, mid)):
                    coef[i, l + d, tile(s), :] = x

    def sweep(k, G):
        def side(l, j, dy, sy):
            side_vel(k, G, l, j, dy, sy)

        def new(l, dy, sy):
            if k < SWEEPS:
                new_vel(k, l, dy, sy)
            else:
                new_heat(l, dy)

        def pack(l, j):
            if k < SWEEPS:
                pack_vel(k + 1, G, l, j)

        side(*start_of(G, 0), dya, sya)

        def body(i, c):
            l, j = start_of(G, i)
            lb, jb = start_of(G, jnp.maximum(i - 1, 0))
            ln, jn = start_of(G, i + 1)
            pack(lb + UB, jb + UB)
            new(l, dya, sya)
            side(l + UB, j + UB, dyb, syb)
            pack(l, j)
            new(l + UB, dyb, syb)
            side(ln, jn, dya, sya)
            return c

        lax.fori_loop(0, HB, body, 0)
        l, j = start_of(G, HB - 1)
        pack(l + UB, j + UB)

    def pack_th(k, G, l):
        for d in range(UT):
            hit = pair == l + d
            for s in range(NS):
                pltpu.store(
                    tpk.at[k, G, tile(s), :],
                    roll(T[k % 2][l + d + 1, rows(s), :], 2 * (l + d) + 1),
                    mask=hit,
                )

    def blocks(segs):
        counts = [-(-(b - a) // UT) for a, b in segs]
        total = sum(counts) + sum(counts) % 2

        def start(i):
            i = jnp.minimum(i, sum(counts) - 1)
            if len(segs) == 1:
                (a, b), = segs
                return jnp.minimum(a + i * UT, b - UT)
            (a, b), (c, e) = segs
            return jnp.where(
                i < counts[0],
                jnp.minimum(a + i * UT, b - UT),
                jnp.minimum(c + (i - counts[0]) * UT, e - UT),
            )

        return total, start

    def theta_first(G):
        total, start = blocks(th_segs(0, G))

        def body(i, c):
            pack_th(0, G, start(i))
            return c

        lax.fori_loop(0, total, body, 0)

    def th_merge(k, G):
        for s in range(NS):
            w = jnp.where(odd, trx[k, G, 1, tile(s), :], roll(trx[k, G, 0, tile(s), :], 2))
            if G == I:
                (a, b), = th_segs(k, I)
                mine = jnp.logical_and(lane > 2 * a, lane <= 2 * b)
                w = jnp.where(mine, w, tmg[k, tile(s), :])
            tmg[k, tile(s), :] = w

    def side_th(k, l, ns):
        for d in range(UT):
            to = LANES - 2 - 2 * (l + d)
            for s in range(NS):
                x = T[k % 2][l + d + 1, rows(s), :]
                edge = roll(tmg[k, tile(s), :], to)
                ns[0, d, tile(s), :] = jnp.where(last, edge, roll(x, LANES - 1))
                ns[1, d, tile(s), :] = jnp.where(first, edge, roll(x, 1))

    def new_th(k, l, ns):
        V = T[k % 2]
        for d in range(UT):
            x = l + d
            for s in range(NS):
                q, west, east, south, north, mid = [coef[i, x, tile(s), :] for i in range(6)]
                value = (
                    (mid * V[x + 1, rows(s), :] + 0.2 * (V[x + 2, rows(s), :] + V[x, rows(s), :]))
                    + (west * V[x + 1, rows(s, -1), :] + east * V[x + 1, rows(s, 1), :])
                    + ((south * ns[1, d, tile(s), :] + north * ns[0, d, tile(s), :]) + q)
                )
                if k < SECTIONS - 1:
                    T[(k + 1) % 2][x + 1, rows(s), :] = value
                else:
                    temp_st[x, tile(s), :] = value
                    hard_st[x, tile(s), :] = jnp.exp(-0.6 * value)

    def section(k, G):
        total, start = blocks(th_segs(k + 1, G))

        def pack(l):
            if k < SECTIONS - 1:
                pack_th(k + 1, G, l)

        side_th(k, start(0), nsa)

        def body(i, c):
            l, lm, ln = start(2 * i), start(2 * i + 1), start(2 * i + 2)
            pack(start(jnp.maximum(2 * i - 1, 0)))
            new_th(k, l, nsa)
            side_th(k, lm, nsb)
            pack(l)
            new_th(k, lm, nsb)
            side_th(k, ln, nsa)
            return c

        lax.fori_loop(0, total // 2, body, 0)
        pack(start(total - 1))

    def temp_move(i):
        q, a, b = segs_out[i][1:]
        src = temp_st.at[a:b]
        dst = temp_out.at[
            a - q * LG : b - q * LG, :, pl.ds(pl.multiple_of(g * LANES, LANES), LANES)
        ]
        far = pltpu.make_async_remote_copy(
            src, dst, os_sem.at[i], or_sem.at[i, g], device_id=(t, q), device_id_type=MESH
        )
        return far, pltpu.make_async_copy(src, dst, os_sem.at[i])

    def temp_send(i):
        q = segs_out[i][1]

        @pl.when(g != q)
        def _():
            temp_move(i)[0].start()

        @pl.when(g == q)
        def _():
            temp_move(i)[1].start()

    def temp_wait(i):
        q, a, b = segs_out[i][1:]

        @pl.when(g != q)
        def _():
            temp_move(i)[0].wait_send()

        @pl.when(g == q)
        def _():
            temp_move(i)[1].wait()
            for src in range(m):
                if src != q:
                    dst = temp_out.at[
                        a - q * LG : b - q * LG, :, src * LANES : (src + 1) * LANES
                    ]
                    pltpu.make_async_remote_copy(
                        dst, dst, os_sem.at[i], or_sem.at[i, src],
                        device_id=(t, g), device_id_type=MESH,
                    ).wait_recv()

    for G in (O, I):
        send(vel_moves(0, G, "row"))
    bulk(0)
    for G in (O, I):
        for cp in vel_cp[G]:
            cp.wait()
        pack_first(G)
        send(vel_moves(0, G, "col"))
    bulk(1)
    ice = icy[...].astype(f32)
    water = (1.0 - ice) * (1.0 / FOLD)
    cb[0] = ice * grav[0] * (1.0 / FOLD)
    cb[1] = ice * grav[1] * (1.0 / FOLD)
    cb[2] = water + slide[...] * bed[...].astype(f32) * (1.0 / FOLD)
    cb[3] = water
    cb[4] = ice
    rate_cp.wait()

    def ice_rate(i, c):
        for d in range(UT):
            for s in range(NS):
                rate[i * UT + d, tile(s), :] = rate[i * UT + d, tile(s), :] * cb[4, tile(s), :]
        return c

    lax.fori_loop(0, L // UT, ice_rate, 0)

    vel_back = {
        G: [
            pltpu.make_async_copy(
                U[SWEEPS % 2].at[:, a:b, PAD:TOP, :], vel_out.at[:, a:b], hs_sem.at[2 * G + i]
            )
            for i, (a, b) in enumerate(SEGS[G])
        ]
        for G in (O, I)
    }
    for k in range(SWEEPS):
        for G in (O, I):
            received(vel_moves(k, G, "all"))
            if k:
                sent(vel_moves(k - 1, G, "all"))
            merge(k, G)
            sweep(k, G)
            send(vel_moves(k + 1, G, "all"))
            bulk(2 + 2 * k + G)
            if k == SWEEPS - 1:
                for cp in vel_back[G]:
                    cp.start()

    def owners(G):
        return sorted({q for q in range(m) for a, b in th_segs(0, G) if a < (q + 1) * LG and b > q * LG})

    def heat_part(G):
        received(vel_moves(SWEEPS, G, "all"))
        merge(SWEEPS, G)
        sweep(SWEEPS, G)

    def th_part(k, G):
        received(th_moves(k, G))
        th_merge(k, G)
        if k:
            sent(th_moves(k - 1, G))
        section(k, G)
        if k < SECTIONS - 1:
            send(th_moves(k + 1, G))
        else:
            for i, sg in enumerate(segs_out):
                if sg[0] == G:
                    temp_send(i)
            for cp in hard_back[G]:
                cp.start()

    def th_start(G, known=()):
        warm_arrived([q for q in owners(G) if q not in known])
        theta_first(G)
        send(th_moves(0, G))

    hard_back = {
        G: [
            pltpu.make_async_copy(hard_st.at[a:b], hard_out.at[a:b], hs_sem.at[4 + 2 * G + i])
            for i, (a, b) in enumerate(th_segs(SECTIONS, G))
        ]
        for G in (O, I)
    }
    th_start(O)
    heat_part(O)
    th_part(0, O)
    heat_part(I)
    th_start(I, owners(O))
    th_part(1, O)
    th_part(0, I)
    th_part(2, O)
    th_part(1, I)
    th_part(3, O)
    th_part(2, I)
    th_part(3, I)

    for i in range(len(segs_out)):
        temp_wait(i)
    warm_sent()
    for G in (O, I):
        for cp in vel_back[G] + hard_back[G]:
            cp.wait()
        sent(vel_moves(SWEEPS - 1, G, "all"))
        sent(vel_moves(SWEEPS, G, "all"))
        sent(th_moves(SECTIONS - 1, G))


def local(n, m, vel, rate, warm, grav, slide, icy, bed):
    _, L, R, Y = vel.shape
    LG = L // m
    assert Y == LANES and R % SUB == 0 and L % (16 * UB) == 0 and LG % PL == 0
    assert 2 * L == LANES and L // 4 >= SECTIONS + UT
    f32 = jnp.float32
    Q = L // 4
    cut = SECTIONS
    parts = [(0, 0, Q - cut), (0, L - Q + cut, L), (1, Q - cut, L - Q + cut)]
    segs_out = []
    for G, a, b in parts:
        while a < b:
            q = a // LG
            e = min(b, (q + 1) * LG)
            segs_out.append((G, q, a, e))
            a = e
    segs_out = tuple(segs_out)
    any_spec = pl.BlockSpec(memory_space=pl.ANY)
    vmem = pl.BlockSpec(memory_space=pltpu.VMEM)
    K = SWEEPS + 1
    H = R + 2 * PAD
    V = pltpu.VMEM
    dma = pltpu.SemaphoreType.DMA
    return pl.pallas_call(
        functools.partial(kernel, n, m, R, L, LG, segs_out),
        out_shape=(
            jax.ShapeDtypeStruct(vel.shape, f32),
            jax.ShapeDtypeStruct(warm.shape, f32),
            jax.ShapeDtypeStruct(rate.shape, f32),
        ),
        in_specs=[any_spec] * 3 + [vmem] * 4,
        out_specs=(any_spec,) * 3,
        scratch_shapes=[
            V((2, L, H, LANES), f32),
            V((2, L, H, LANES), f32),
            V((L + 2, H, LANES), f32),
            V((L + 2, H, LANES), f32),
            V((L, R, LANES), f32),
            V((6, L, R, LANES), f32),
            V((L, R, LANES), f32),
            V((L, R, LANES), f32),
            V((5, R, LANES), f32),
            V((2, UB, H, LANES), f32),
            V((2, UB, H, LANES), f32),
            V((2, UB, R, LANES), f32),
            V((2, UB, R, LANES), f32),
            V((2, UT, R, LANES), f32),
            V((2, UT, R, LANES), f32),
            V((K, 2, H, LANES), f32),
            V((K, 2, 2, H, LANES), f32),
            V((2, H, LANES), f32),
            V((SECTIONS, 2, R, LANES), f32),
            V((SECTIONS, 2, 2, R, LANES), f32),
            V((SECTIONS, R, LANES), f32),
            dma((6,)),
            dma((K, 2, 10)),
            dma((K, 2, 10)),
            dma((SECTIONS, 2, 6)),
            dma((SECTIONS, 2, 6)),
            dma,
            dma((m,)),
            dma((len(segs_out),)),
            dma((len(segs_out), m)),
            dma((8,)),
        ],
        compiler_params=pltpu.CompilerParams(
            collective_id=0, has_side_effects=True, vmem_limit_bytes=60 * 1024 * 1024
        ),
        name="ice_step",
    )(vel, rate, warm, grav, slide, icy, bed)


def solution(mesh):
    return jax.shard_map(
        functools.partial(local, mesh.shape["tile"], mesh.shape["grp"]),
        mesh=mesh,
        in_specs=(
            P(None, None, "tile", "grp"),
            P(None, "tile", "grp"),
            P("grp", "tile", None),
            P(None, "tile", "grp"),
            P("tile", "grp"),
            P("tile", "grp"),
            P("tile", "grp"),
        ),
        out_specs=(P(None, None, "tile", "grp"), P("grp", "tile", None), P(None, "tile", "grp")),
        check_vma=False,
    )
```

```python
import functools

import jax
import jax.numpy as jnp
from jax import lax
from jax.experimental import pallas as pl
from jax.experimental.pallas import tpu as pltpu
from jax.sharding import PartitionSpec as P

SWEEPS = 4
SECTIONS = 4
LANES = 128
SUB = 8
PAD = 8
UB = 2
UT = 4
PL = 2
OUT_STEP = 2
IN_START = 40

MESH = pl.DeviceIdType.MESH
FOLD = 4.0 ** (1.0 / 3.0)


def roll(x, shift):
    return pltpu.roll(x, shift, 1)


def kernel(
    n,
    m,
    R,
    L,
    LG,
    segs_out,
    vel_in,
    rate_in,
    warm_in,
    grav,
    slide,
    icy,
    bed,
    vel_out,
    temp_out,
    hard_out,
    U0,
    U1,
    T0,
    T1,
    rate,
    coef,
    temp_st,
    hard_st,
    cb,
    dya,
    dyb,
    sya,
    syb,
    nsa,
    nsb,
    pk,
    crx,
    mg,
    tpk,
    trx,
    tmg,
    loc_sem,
    vs_sem,
    vr_sem,
    ts_sem,
    tr_sem,
    ws_sem,
    wr_sem,
    os_sem,
    or_sem,
    hs_sem,
):
    t = lax.axis_index("tile")
    g = lax.axis_index("grp")
    U = (U0, U1)
    T = (T0, T1)
    f32 = jnp.float32
    NS = R // SUB
    TOP = PAD + R
    Q = L // 4
    O, I = 0, 1
    SEGS = {O: ((0, Q), (L - Q, L)), I: ((Q, L - Q),)}

    def th_segs(k, G):
        if G == O:
            return ((0, Q - k), (L - Q + k, L))
        return ((Q - k, L - Q + k),)

    vel_cp = {
        G: [
            pltpu.make_async_copy(
                vel_in.at[:, a:b], U0.at[:, a:b, PAD:TOP, :], loc_sem.at[2 * G + i]
            )
            for i, (a, b) in enumerate(SEGS[G])
        ]
        for G in (O, I)
    }
    rate_cp = pltpu.make_async_copy(rate_in, rate, loc_sem.at[4])
    warm_cp = pltpu.make_async_copy(
        warm_in.at[:, :, pl.ds(pl.multiple_of(g * LANES, LANES), LANES)],
        T0.at[pl.ds(1 + g * LG, LG), PAD:TOP, :],
        loc_sem.at[5],
    )
    for G in (O, I):
        for cp in vel_cp[G]:
            cp.start()
    rate_cp.start()
    warm_cp.start()

    lo_t, hi_t, lo_g, hi_g = t > 0, t < n - 1, g > 0, g < m - 1

    def has(dt, dg):
        ok = None
        for d, lo, hi in ((dt, lo_t, hi_t), (dg, lo_g, hi_g)):
            if d:
                c = lo if d < 0 else hi
                ok = c if ok is None else jnp.logical_and(ok, c)
        return ok

    zero = jnp.zeros((SUB, LANES), f32)

    def clear_rows(l, c):
        for slot in range(2):
            for f in range(2):
                U[slot][f, l, 0:PAD, :] = zero
                U[slot][f, l, TOP : TOP + SUB, :] = zero
            T[slot][l + 1, 0:PAD, :] = zero
            T[slot][l + 1, TOP : TOP + SUB, :] = zero
        return c

    lax.fori_loop(0, L, clear_rows, 0)
    for slot in range(2):
        for l in (0, L + 1):
            T[slot][l] = jnp.zeros_like(T[slot][l])
    crx[...] = jnp.zeros_like(crx)
    trx[...] = jnp.zeros_like(trx)

    barrier = pltpu.get_barrier_semaphore()
    around = [(-1, -1), (-1, 0), (-1, 1), (1, -1), (1, 0), (1, 1)]
    for dt, dg in around:

        @pl.when(has(dt, dg))
        def _(dt=dt, dg=dg):
            pl.semaphore_signal(
                barrier, inc=1, device_id=(t + dt, g + dg), device_id_type=MESH
            )

    for d in range(1, m):
        pl.semaphore_signal(
            barrier, inc=1, device_id=(t, lax.rem(g + d, m)), device_id_type=MESH
        )

    sides_t = lo_t.astype(jnp.int32) + hi_t.astype(jnp.int32)
    sides_g = lo_g.astype(jnp.int32) + hi_g.astype(jnp.int32)
    pl.semaphore_wait(barrier, m - 1 + sides_t * (1 + sides_g))

    def vel_moves(k, G, part):
        slot = k % 2
        moves = []
        if part != "col":
            for a, b in SEGS[G]:
                if k == 0:
                    top, low = vel_in.at[:, a:b, R - 1, :], vel_in.at[:, a:b, 0, :]
                else:
                    top = U[slot].at[:, a:b, TOP - 1, :]
                    low = U[slot].at[:, a:b, PAD, :]
                moves += [
                    ((1, 0), top, U[slot].at[:, a:b, PAD - 1, :]),
                    ((-1, 0), low, U[slot].at[:, a:b, TOP, :]),
                ]
        if part != "row":
            moves += [
                ((0, 1), pk.at[k, G, PAD:TOP], crx.at[k, G, 0, PAD:TOP]),
                ((0, -1), pk.at[k, G, PAD:TOP], crx.at[k, G, 1, PAD:TOP]),
            ]
            if k < SWEEPS:
                for dg, side in ((1, 0), (-1, 1)):
                    moves += [
                        ((1, dg), pk.at[k, G, TOP - 1], crx.at[k, G, side, PAD - 1]),
                        ((-1, dg), pk.at[k, G, PAD], crx.at[k, G, side, TOP]),
                    ]
        first = 4 if part == "col" else 0
        if part == "all":
            rows = 2 * len(SEGS[G])
            index = list(range(rows)) + list(range(4, 4 + len(moves) - rows))
        else:
            index = list(range(first, first + len(moves)))
        return [
            (mv, vs_sem.at[k, G, j], vr_sem.at[k, G, j]) for mv, j in zip(moves, index)
        ]

    def th_moves(k, G):
        slot = k % 2
        moves = []
        for a, b in th_segs(k, G):
            moves += [
                ((1, 0), T[slot].at[1 + a : 1 + b, TOP - 1, :], T[slot].at[1 + a : 1 + b, PAD - 1, :]),
                ((-1, 0), T[slot].at[1 + a : 1 + b, PAD, :], T[slot].at[1 + a : 1 + b, TOP, :]),
            ]
        moves += [
            ((0, 1), tpk.at[k, G], trx.at[k, G, 0]),
            ((0, -1), tpk.at[k, G], trx.at[k, G, 1]),
        ]
        return [(mv, ts_sem.at[k, G, j], tr_sem.at[k, G, j]) for j, mv in enumerate(moves)]

    def remote(mv, s_sem, r_sem, sign=1):
        (dt, dg), src, dst = mv
        return pltpu.make_async_remote_copy(
            src,
            dst,
            s_sem,
            r_sem,
            device_id=(t + sign * dt, g + sign * dg),
            device_id_type=MESH,
        )

    def send(moves):
        for mv, s_sem, r_sem in moves:

            @pl.when(has(*mv[0]))
            def _(mv=mv, s_sem=s_sem, r_sem=r_sem):
                remote(mv, s_sem, r_sem).start()

    def sent(moves):
        for mv, s_sem, r_sem in moves:

            @pl.when(has(*mv[0]))
            def _(mv=mv, s_sem=s_sem, r_sem=r_sem):
                remote(mv, s_sem, r_sem).wait_send()

    def received(moves):
        for mv, s_sem, r_sem in moves:
            dt, dg = mv[0]

            @pl.when(has(-dt, -dg))
            def _(mv=mv, s_sem=s_sem, r_sem=r_sem):
                remote(mv, s_sem, r_sem, -1).wait_recv()

    up_half = 2 * g < m

    def target(i):
        asc = i + (i >= g).astype(jnp.int32)
        x = m - 1 - i
        desc = x - (x <= g).astype(jnp.int32)
        return jnp.where(up_half, desc, asc)

    def warm_piece(i, p):
        to = target(i)
        return pltpu.make_async_remote_copy(
            warm_in.at[pl.ds(p * PL, PL), :, pl.ds(pl.multiple_of(to * LANES, LANES), LANES)],
            T0.at[pl.ds(1 + g * LG + p * PL, PL), PAD:TOP, :],
            ws_sem,
            wr_sem.at[g],
            device_id=(t, to),
            device_id_type=MESH,
        )

    def warm_recv(src):
        part = T0.at[1 + src * LG : 1 + (src + 1) * LG, PAD:TOP, :]
        return pltpu.make_async_remote_copy(
            part, part, ws_sem, wr_sem.at[src], device_id=(t, g), device_id_type=MESH
        )

    def warm_sent():
        part = temp_st.at[0 : (m - 1) * LG]
        pltpu.make_async_remote_copy(
            part, part, ws_sem, wr_sem.at[0], device_id=(t, g), device_id_type=MESH
        ).wait_send()

    outer = jnp.logical_or(g * LG < Q, (g + 1) * LG > L - Q)
    NP = LG // PL
    COUNT = (m - 1) * NP

    def feed(c):
        far = (m - 2) * NP

        @pl.when(jnp.logical_and(outer, jnp.logical_and(lax.rem(c, OUT_STEP) == 0, c < OUT_STEP * COUNT)))
        def _():
            q = lax.div(c, OUT_STEP)
            near = q >= far
            i = jnp.where(near, m - 2, lax.rem(q, m - 2))
            warm_piece(i, jnp.where(near, q - far, lax.div(q, m - 2))).start()

        @pl.when(
            jnp.logical_and(
                jnp.logical_not(outer), jnp.logical_and(c >= IN_START, c < IN_START + COUNT)
            )
        )
        def _():
            q = c - IN_START
            warm_piece(lax.rem(q, m - 1), lax.div(q, m - 1)).start()

    def warm_arrived(sources):
        for src in sources:

            @pl.when(g == src)
            def _():
                warm_cp.wait()

            @pl.when(g != src)
            def _(src=src):
                warm_recv(src).wait_recv()

    lane = lax.broadcasted_iota(jnp.int32, (SUB, LANES), 1)
    first = lane == 0
    last = lane == LANES - 1
    odd = lax.rem(lane, 2) == 1
    pair = lax.div(lane, 2)
    bottom = lax.broadcasted_iota(jnp.int32, (SUB, LANES), 0) == SUB - 1

    def rows(s, d=0):
        return slice(PAD + s * SUB + d, PAD + s * SUB + d + SUB)

    def tile(s):
        return slice(s * SUB, (s + 1) * SUB)

    HB = L // 2 // (2 * UB)

    def start_of(G, i):
        i = jnp.minimum(i, HB - 1) * (2 * UB)
        if G == I:
            return i + Q, i
        return i + jnp.where(i >= Q, L // 2, 0), i

    def edge_spot(j):
        return (
            lax.rem(2 * LANES - 2 - 2 * j, LANES),
            lax.rem(2 * LANES - 2 - LANES // 2 - 2 * j, LANES),
        )

    def pack_spot(j):
        return (
            (pair == j, 2 * j + 1),
            (pair == j + LANES // 4, lax.rem(2 * j + LANES // 2 + 1, LANES)),
        )

    def pack_vel(k, G, l, j):
        for d in range(UB):
            sp = pack_spot(j + d)
            for s in range(NS):
                for f in range(2):
                    hit, to = sp[f]
                    pltpu.store(
                        pk.at[k, G, rows(s), :],
                        roll(U[k % 2][f, l + d, rows(s), :], to),
                        mask=hit,
                    )

    def pack_first(G):
        def body(i, c):
            l, j = start_of(G, i)
            pack_vel(0, G, l, j)
            pack_vel(0, G, l + UB, j + UB)
            return c

        lax.fori_loop(0, HB, body, 0)

    def merge(k, G):
        for s in range(-1, NS + 1):
            w = jnp.where(odd, crx[k, G, 1, rows(s), :], roll(crx[k, G, 0, rows(s), :], 2))
            mg[G, rows(s), :] = w
            if s == -1:
                low = w
        mg[G, rows(NS), :] = jnp.where(bottom, low, w)

    def side_vel(k, G, l, j, dy, sy):
        V = U[k % 2]
        tiles = NS + 1 if k < SWEEPS else NS
        for d in range(UB):
            sp = edge_spot(j + d)
            for s in range(tiles):
                halo = mg[G, rows(s), :]
                for f in range(2):
                    x = V[f, l + d, rows(s), :]
                    if s == NS:
                        x = jnp.where(bottom, V[f, l + d, rows(-1), :], x)
                    edge = roll(halo, sp[f])
                    up = jnp.where(last, edge, roll(x, LANES - 1))
                    down = jnp.where(first, edge, roll(x, 1))
                    diff = up - down
                    dy[f, d, rows(s), :] = diff
                    if s == NS:
                        dy[f, d, rows(-1), :] = diff
                    elif k < SWEEPS:
                        sy[f, d, tile(s), :] = up + down

    def strain(slot, l, d, s, dy):
        l = l + d
        lm = jnp.maximum(l - 1, 0)
        lp = jnp.minimum(l + 1, L - 1)
        V = U[slot]
        e, w, up, lo = [], [], [], []
        for f in range(2):
            e.append(V[f, l, rows(s, 1), :])
            w.append(V[f, l, rows(s, -1), :])
            up.append(V[f, lp, rows(s), :])
            lo.append(V[f, lm, rows(s), :])
        xu, xv = e[0] - w[0], e[1] - w[1]
        yv = dy[1, d, rows(s), :]
        shear = dy[0, d, rows(s), :] + xv
        du, dv = up[0] - lo[0], up[1] - lo[1]
        total = (xu * (xu + yv) + yv * yv) + 0.25 * (
            (shear * shear + du * du) + dv * dv
        )
        visc = rate[l, tile(s), :] * jnp.exp2(lax.log2(total + 0.04) * (-1.0 / 3.0))
        return e, w, up, lo, total, visc

    def new_vel(k, l, dy, sy):
        slot, new_slot = k % 2, (k + 1) % 2
        for d in range(UB):
            low = jnp.minimum(l + d, 1)
            for s in range(NS):
                e, w, up, lo, _, visc = strain(slot, l, d, s, dy)
                cross_u = dy[1, d, rows(s, 1), :] - dy[1, d, rows(s, -1), :]
                cross_v = dy[0, d, rows(s, 1), :] - dy[0, d, rows(s, -1), :]
                near_u = (
                    4.0 * ((e[0] + w[0]) + (up[0] + lo[0]))
                    + sy[0, d, tile(s), :]
                    + 0.75 * cross_u
                )
                near_v = (
                    4.0 * (sy[1, d, tile(s), :] + (up[1] + lo[1]))
                    + (e[1] + w[1])
                    + 0.75 * cross_v
                )
                scale = 1.0 / (22.0 * visc + cb[2 + low, tile(s), :])
                U[new_slot][0, l + d, rows(s), :] = (cb[0, tile(s), :] + visc * near_u) * scale
                U[new_slot][1, l + d, rows(s), :] = (cb[1, tile(s), :] + visc * near_v) * scale

    def new_heat(l, dy):
        slot = SWEEPS % 2
        for d in range(UB):
            for s in range(NS):
                *_, total, visc = strain(slot, l, d, s, dy)
                q = (0.025 * FOLD) * (visc * total)
                u = 0.05 * U[slot][0, l + d, rows(s), :]
                v = 0.05 * U[slot][1, l + d, rows(s), :]
                west = 0.1 + jnp.maximum(u, 0.0)
                east = 0.1 - jnp.minimum(u, 0.0)
                south = 0.1 + jnp.maximum(v, 0.0)
                north = 0.1 - jnp.minimum(v, 0.0)
                mid = 0.6 - ((west + east) + (south + north))
                for i, x in enumerate((q, west, east, south, north, mid)):
                    coef[i, l + d, tile(s), :] = x

    def sweep(k, G):
        def side(l, j, dy, sy):
            side_vel(k, G, l, j, dy, sy)

        def new(l, dy, sy):
            if k < SWEEPS:
                new_vel(k, l, dy, sy)
            else:
                new_heat(l, dy)

        def pack(l, j):
            if k < SWEEPS:
                pack_vel(k + 1, G, l, j)

        side(*start_of(G, 0), dya, sya)

        def body(i, c):
            l, j = start_of(G, i)
            lb, jb = start_of(G, jnp.maximum(i - 1, 0))
            ln, jn = start_of(G, i + 1)
            if k < SWEEPS:
                feed((2 * k + G) * HB + i)
            pack(lb + UB, jb + UB)
            new(l, dya, sya)
            side(l + UB, j + UB, dyb, syb)
            pack(l, j)
            new(l + UB, dyb, syb)
            side(ln, jn, dya, sya)
            return c

        lax.fori_loop(0, HB, body, 0)
        l, j = start_of(G, HB - 1)
        pack(l + UB, j + UB)

    def pack_th(k, G, l):
        for d in range(UT):
            hit = pair == l + d
            for s in range(NS):
                pltpu.store(
                    tpk.at[k, G, tile(s), :],
                    roll(T[k % 2][l + d + 1, rows(s), :], 2 * (l + d) + 1),
                    mask=hit,
                )

    def blocks(segs):
        counts = [-(-(b - a) // UT) for a, b in segs]
        total = sum(counts) + sum(counts) % 2

        def start(i):
            i = jnp.minimum(i, sum(counts) - 1)
            if len(segs) == 1:
                (a, b), = segs
                return jnp.minimum(a + i * UT, b - UT)
            (a, b), (c, e) = segs
            return jnp.where(
                i < counts[0],
                jnp.minimum(a + i * UT, b - UT),
                jnp.minimum(c + (i - counts[0]) * UT, e - UT),
            )

        return total, start

    def theta_first(G):
        total, start = blocks(th_segs(0, G))

        def body(i, c):
            pack_th(0, G, start(i))
            return c

        lax.fori_loop(0, total, body, 0)

    def th_merge(k, G):
        for s in range(NS):
            w = jnp.where(odd, trx[k, G, 1, tile(s), :], roll(trx[k, G, 0, tile(s), :], 2))
            if G == I:
                (a, b), = th_segs(k, I)
                mine = jnp.logical_and(lane > 2 * a, lane <= 2 * b)
                w = jnp.where(mine, w, tmg[k, tile(s), :])
            tmg[k, tile(s), :] = w

    def side_th(k, l, ns):
        for d in range(UT):
            to = LANES - 2 - 2 * (l + d)
            for s in range(NS):
                x = T[k % 2][l + d + 1, rows(s), :]
                edge = roll(tmg[k, tile(s), :], to)
                ns[0, d, tile(s), :] = jnp.where(last, edge, roll(x, LANES - 1))
                ns[1, d, tile(s), :] = jnp.where(first, edge, roll(x, 1))

    def new_th(k, l, ns):
        V = T[k % 2]
        for d in range(UT):
            x = l + d
            for s in range(NS):
                q, west, east, south, north, mid = [coef[i, x, tile(s), :] for i in range(6)]
                value = (
                    (mid * V[x + 1, rows(s), :] + 0.2 * (V[x + 2, rows(s), :] + V[x, rows(s), :]))
                    + (west * V[x + 1, rows(s, -1), :] + east * V[x + 1, rows(s, 1), :])
                    + ((south * ns[1, d, tile(s), :] + north * ns[0, d, tile(s), :]) + q)
                )
                if k < SECTIONS - 1:
                    T[(k + 1) % 2][x + 1, rows(s), :] = value
                else:
                    temp_st[x, tile(s), :] = value
                    hard_st[x, tile(s), :] = jnp.exp(-0.6 * value)

    def section(k, G):
        total, start = blocks(th_segs(k + 1, G))

        def pack(l):
            if k < SECTIONS - 1:
                pack_th(k + 1, G, l)

        side_th(k, start(0), nsa)

        def body(i, c):
            l, lm, ln = start(2 * i), start(2 * i + 1), start(2 * i + 2)
            pack(start(jnp.maximum(2 * i - 1, 0)))
            new_th(k, l, nsa)
            side_th(k, lm, nsb)
            pack(l)
            new_th(k, lm, nsb)
            side_th(k, ln, nsa)
            return c

        lax.fori_loop(0, total // 2, body, 0)
        pack(start(total - 1))

    def temp_move(i):
        q, a, b = segs_out[i][1:]
        src = temp_st.at[a:b]
        dst = temp_out.at[
            a - q * LG : b - q * LG, :, pl.ds(pl.multiple_of(g * LANES, LANES), LANES)
        ]
        far = pltpu.make_async_remote_copy(
            src, dst, os_sem.at[i], or_sem.at[i, g], device_id=(t, q), device_id_type=MESH
        )
        return far, pltpu.make_async_copy(src, dst, os_sem.at[i])

    def temp_send(i):
        q = segs_out[i][1]

        @pl.when(g != q)
        def _():
            temp_move(i)[0].start()

        @pl.when(g == q)
        def _():
            temp_move(i)[1].start()

    def temp_wait(i):
        q, a, b = segs_out[i][1:]

        @pl.when(g != q)
        def _():
            temp_move(i)[0].wait_send()

        @pl.when(g == q)
        def _():
            temp_move(i)[1].wait()
            for src in range(m):
                if src != q:
                    dst = temp_out.at[
                        a - q * LG : b - q * LG, :, src * LANES : (src + 1) * LANES
                    ]
                    pltpu.make_async_remote_copy(
                        dst, dst, os_sem.at[i], or_sem.at[i, src],
                        device_id=(t, g), device_id_type=MESH,
                    ).wait_recv()

    for G in (O, I):
        send(vel_moves(0, G, "row"))
    for G in (O, I):
        for cp in vel_cp[G]:
            cp.wait()
        pack_first(G)
        send(vel_moves(0, G, "col"))
    ice = icy[...].astype(f32)
    water = (1.0 - ice) * (1.0 / FOLD)
    cb[0] = ice * grav[0] * (1.0 / FOLD)
    cb[1] = ice * grav[1] * (1.0 / FOLD)
    cb[2] = water + slide[...] * bed[...].astype(f32) * (1.0 / FOLD)
    cb[3] = water
    cb[4] = ice
    rate_cp.wait()

    def ice_rate(i, c):
        for d in range(UT):
            for s in range(NS):
                rate[i * UT + d, tile(s), :] = rate[i * UT + d, tile(s), :] * cb[4, tile(s), :]
        return c

    lax.fori_loop(0, L // UT, ice_rate, 0)

    vel_back = {
        G: [
            pltpu.make_async_copy(
                U[SWEEPS % 2].at[:, a:b, PAD:TOP, :], vel_out.at[:, a:b], hs_sem.at[2 * G + i]
            )
            for i, (a, b) in enumerate(SEGS[G])
        ]
        for G in (O, I)
    }
    def owners(G):
        return sorted({q for q in range(m) for a, b in th_segs(0, G) if a < (q + 1) * LG and b > q * LG})

    def heat_part(G):
        received(vel_moves(SWEEPS, G, "all"))
        merge(SWEEPS, G)
        sweep(SWEEPS, G)

    def th_part(k, G):
        received(th_moves(k, G))
        th_merge(k, G)
        if k:
            sent(th_moves(k - 1, G))
        section(k, G)
        if k < SECTIONS - 1:
            send(th_moves(k + 1, G))
        else:
            for cp in hard_back[G]:
                cp.start()

    def th_start(G, known=()):
        warm_arrived([q for q in owners(G) if q not in known])
        theta_first(G)
        send(th_moves(0, G))

    hard_back = {
        G: [
            pltpu.make_async_copy(hard_st.at[a:b], hard_out.at[a:b], hs_sem.at[4 + 2 * G + i])
            for i, (a, b) in enumerate(th_segs(SECTIONS, G))
        ]
        for G in (O, I)
    }

    def temp_out_part(G):
        for i, sg in enumerate(segs_out):
            if sg[0] == G:
                temp_send(i)

    for k in range(SWEEPS):
        for G in (O, I):
            received(vel_moves(k, G, "all"))
            if k:
                sent(vel_moves(k - 1, G, "all"))
            merge(k, G)
            sweep(k, G)
            send(vel_moves(k + 1, G, "all"))
            if k == SWEEPS - 1:
                for cp in vel_back[G]:
                    cp.start()
                if G == O:
                    th_start(O)

    heat_part(O)
    th_part(0, O)
    th_start(I, owners(O))
    heat_part(I)
    th_part(1, O)
    th_part(0, I)
    th_part(2, O)
    th_part(1, I)
    th_part(3, O)
    th_part(2, I)
    temp_out_part(O)
    th_part(3, I)
    temp_out_part(I)

    for i in range(len(segs_out)):
        temp_wait(i)
    warm_sent()
    for G in (O, I):
        for cp in vel_back[G] + hard_back[G]:
            cp.wait()
        sent(vel_moves(SWEEPS - 1, G, "all"))
        sent(vel_moves(SWEEPS, G, "all"))
        sent(th_moves(SECTIONS - 1, G))


def local(n, m, vel, rate, warm, grav, slide, icy, bed):
    _, L, R, Y = vel.shape
    LG = L // m
    assert Y == LANES and R % SUB == 0 and L % (16 * UB) == 0 and LG % PL == 0 and m > 2
    assert IN_START + (m - 1) * LG // PL <= SWEEPS * L // (2 * UB)
    assert 2 * L == LANES and L // 4 >= SECTIONS + UT
    f32 = jnp.float32
    Q = L // 4
    cut = SECTIONS
    parts = [(0, 0, Q - cut), (0, L - Q + cut, L), (1, Q - cut, L - Q + cut)]
    segs_out = []
    for G, a, b in parts:
        while a < b:
            q = a // LG
            e = min(b, (q + 1) * LG)
            segs_out.append((G, q, a, e))
            a = e
    segs_out = tuple(segs_out)
    any_spec = pl.BlockSpec(memory_space=pl.ANY)
    vmem = pl.BlockSpec(memory_space=pltpu.VMEM)
    K = SWEEPS + 1
    H = R + 2 * PAD
    V = pltpu.VMEM
    dma = pltpu.SemaphoreType.DMA
    return pl.pallas_call(
        functools.partial(kernel, n, m, R, L, LG, segs_out),
        out_shape=(
            jax.ShapeDtypeStruct(vel.shape, f32),
            jax.ShapeDtypeStruct(warm.shape, f32),
            jax.ShapeDtypeStruct(rate.shape, f32),
        ),
        in_specs=[any_spec] * 3 + [vmem] * 4,
        out_specs=(any_spec,) * 3,
        scratch_shapes=[
            V((2, L, H, LANES), f32),
            V((2, L, H, LANES), f32),
            V((L + 2, H, LANES), f32),
            V((L + 2, H, LANES), f32),
            V((L, R, LANES), f32),
            V((6, L, R, LANES), f32),
            V((L, R, LANES), f32),
            V((L, R, LANES), f32),
            V((5, R, LANES), f32),
            V((2, UB, H, LANES), f32),
            V((2, UB, H, LANES), f32),
            V((2, UB, R, LANES), f32),
            V((2, UB, R, LANES), f32),
            V((2, UT, R, LANES), f32),
            V((2, UT, R, LANES), f32),
            V((K, 2, H, LANES), f32),
            V((K, 2, 2, H, LANES), f32),
            V((2, H, LANES), f32),
            V((SECTIONS, 2, R, LANES), f32),
            V((SECTIONS, 2, 2, R, LANES), f32),
            V((SECTIONS, R, LANES), f32),
            dma((6,)),
            dma((K, 2, 10)),
            dma((K, 2, 10)),
            dma((SECTIONS, 2, 6)),
            dma((SECTIONS, 2, 6)),
            dma,
            dma((m,)),
            dma((len(segs_out),)),
            dma((len(segs_out), m)),
            dma((8,)),
        ],
        compiler_params=pltpu.CompilerParams(
            collective_id=0, has_side_effects=True, vmem_limit_bytes=60 * 1024 * 1024
        ),
        name="ice_step",
    )(vel, rate, warm, grav, slide, icy, bed)


def solution(mesh):
    return jax.shard_map(
        functools.partial(local, mesh.shape["tile"], mesh.shape["grp"]),
        mesh=mesh,
        in_specs=(
            P(None, None, "tile", "grp"),
            P(None, "tile", "grp"),
            P("grp", "tile", None),
            P(None, "tile", "grp"),
            P("tile", "grp"),
            P("tile", "grp"),
            P("tile", "grp"),
        ),
        out_specs=(P(None, None, "tile", "grp"), P("grp", "tile", None), P(None, "tile", "grp")),
        check_vma=False,
    )
```

```python
import functools

import jax
import jax.numpy as jnp
from jax import lax
from jax.experimental import pallas as pl
from jax.experimental.pallas import tpu as pltpu
from jax.sharding import PartitionSpec as P

SWEEPS = 4
SECTIONS = 4
LANES = 128
SUB = 8
PAD = 8
UB = 2
UT = 4
PL = 1
PARTS = 2

MESH = pl.DeviceIdType.MESH
FOLD = 4.0 ** (1.0 / 3.0)


def roll(x, shift):
    return pltpu.roll(x, shift, 1)


def kernel(
    n,
    m,
    R,
    L,
    LG,
    segs_out,
    vel_in,
    rate_in,
    warm_in,
    grav,
    slide,
    icy,
    bed,
    vel_out,
    temp_out,
    hard_out,
    U0,
    U1,
    T0,
    T1,
    rate,
    coef,
    temp_st,
    hard_st,
    cb,
    dya,
    dyb,
    sya,
    syb,
    nsa,
    nsb,
    pk,
    crx,
    mg,
    tpk,
    trx,
    tmg,
    loc_sem,
    vs_sem,
    vr_sem,
    ts_sem,
    tr_sem,
    ws_sem,
    wr_sem,
    os_sem,
    or_sem,
    hs_sem,
):
    t = lax.axis_index("tile")
    g = lax.axis_index("grp")
    U = (U0, U1)
    T = (T0, T1)
    f32 = jnp.float32
    NS = R // SUB
    TOP = PAD + R
    Q = L // 4
    O, I = 0, 1
    SEGS = {O: ((0, Q), (L - Q, L)), I: ((Q, L - Q),)}

    def th_segs(k, G):
        if G == O:
            return ((0, Q - k), (L - Q + k, L))
        return ((Q - k, L - Q + k),)

    vel_cp = {
        G: [
            pltpu.make_async_copy(
                vel_in.at[:, a:b], U0.at[:, a:b, PAD:TOP, :], loc_sem.at[2 * G + i]
            )
            for i, (a, b) in enumerate(SEGS[G])
        ]
        for G in (O, I)
    }
    rate_cp = pltpu.make_async_copy(rate_in, rate, loc_sem.at[4])
    warm_cp = pltpu.make_async_copy(
        warm_in.at[:, :, pl.ds(pl.multiple_of(g * LANES, LANES), LANES)],
        T0.at[pl.ds(1 + g * LG, LG), PAD:TOP, :],
        loc_sem.at[5],
    )
    for G in (O, I):
        for cp in vel_cp[G]:
            cp.start()
    rate_cp.start()
    warm_cp.start()

    lo_t, hi_t, lo_g, hi_g = t > 0, t < n - 1, g > 0, g < m - 1

    def has(dt, dg):
        ok = None
        for d, lo, hi in ((dt, lo_t, hi_t), (dg, lo_g, hi_g)):
            if d:
                c = lo if d < 0 else hi
                ok = c if ok is None else jnp.logical_and(ok, c)
        return ok

    zero = jnp.zeros((SUB, LANES), f32)

    def clear_rows(l, c):
        for slot in range(2):
            for f in range(2):
                U[slot][f, l, 0:PAD, :] = zero
                U[slot][f, l, TOP : TOP + SUB, :] = zero
            T[slot][l + 1, 0:PAD, :] = zero
            T[slot][l + 1, TOP : TOP + SUB, :] = zero
        return c

    lax.fori_loop(0, L, clear_rows, 0)
    for slot in range(2):
        for l in (0, L + 1):
            T[slot][l] = jnp.zeros_like(T[slot][l])
    crx[...] = jnp.zeros_like(crx)
    trx[...] = jnp.zeros_like(trx)

    barrier = pltpu.get_barrier_semaphore()
    around = [(-1, -1), (-1, 0), (-1, 1), (1, -1), (1, 0), (1, 1)]
    for dt, dg in around:

        @pl.when(has(dt, dg))
        def _(dt=dt, dg=dg):
            pl.semaphore_signal(
                barrier, inc=1, device_id=(t + dt, g + dg), device_id_type=MESH
            )

    for d in range(1, m):
        pl.semaphore_signal(
            barrier, inc=1, device_id=(t, lax.rem(g + d, m)), device_id_type=MESH
        )

    sides_t = lo_t.astype(jnp.int32) + hi_t.astype(jnp.int32)
    sides_g = lo_g.astype(jnp.int32) + hi_g.astype(jnp.int32)
    pl.semaphore_wait(barrier, m - 1 + sides_t * (1 + sides_g))

    def vel_moves(k, G, part):
        slot = k % 2
        moves = []
        if part != "col":
            for a, b in SEGS[G]:
                if k == 0:
                    top, low = vel_in.at[:, a:b, R - 1, :], vel_in.at[:, a:b, 0, :]
                else:
                    top = U[slot].at[:, a:b, TOP - 1, :]
                    low = U[slot].at[:, a:b, PAD, :]
                moves += [
                    ((1, 0), top, U[slot].at[:, a:b, PAD - 1, :]),
                    ((-1, 0), low, U[slot].at[:, a:b, TOP, :]),
                ]
        if part != "row":
            moves += [
                ((0, 1), pk.at[k, G, PAD:TOP], crx.at[k, G, 0, PAD:TOP]),
                ((0, -1), pk.at[k, G, PAD:TOP], crx.at[k, G, 1, PAD:TOP]),
            ]
            if k < SWEEPS:
                for dg, side in ((1, 0), (-1, 1)):
                    moves += [
                        ((1, dg), pk.at[k, G, TOP - 1], crx.at[k, G, side, PAD - 1]),
                        ((-1, dg), pk.at[k, G, PAD], crx.at[k, G, side, TOP]),
                    ]
        first = 4 if part == "col" else 0
        if part == "all":
            rows = 2 * len(SEGS[G])
            index = list(range(rows)) + list(range(4, 4 + len(moves) - rows))
        else:
            index = list(range(first, first + len(moves)))
        return [
            (mv, vs_sem.at[k, G, j], vr_sem.at[k, G, j]) for mv, j in zip(moves, index)
        ]

    def th_moves(k, G):
        slot = k % 2
        moves = []
        for a, b in th_segs(k, G):
            moves += [
                ((1, 0), T[slot].at[1 + a : 1 + b, TOP - 1, :], T[slot].at[1 + a : 1 + b, PAD - 1, :]),
                ((-1, 0), T[slot].at[1 + a : 1 + b, PAD, :], T[slot].at[1 + a : 1 + b, TOP, :]),
            ]
        moves += [
            ((0, 1), tpk.at[k, G], trx.at[k, G, 0]),
            ((0, -1), tpk.at[k, G], trx.at[k, G, 1]),
        ]
        return [(mv, ts_sem.at[k, G, j], tr_sem.at[k, G, j]) for j, mv in enumerate(moves)]

    def remote(mv, s_sem, r_sem, sign=1):
        (dt, dg), src, dst = mv
        return pltpu.make_async_remote_copy(
            src,
            dst,
            s_sem,
            r_sem,
            device_id=(t + sign * dt, g + sign * dg),
            device_id_type=MESH,
        )

    def send(moves):
        for mv, s_sem, r_sem in moves:

            @pl.when(has(*mv[0]))
            def _(mv=mv, s_sem=s_sem, r_sem=r_sem):
                remote(mv, s_sem, r_sem).start()

    def sent(moves):
        for mv, s_sem, r_sem in moves:

            @pl.when(has(*mv[0]))
            def _(mv=mv, s_sem=s_sem, r_sem=r_sem):
                remote(mv, s_sem, r_sem).wait_send()

    def received(moves):
        for mv, s_sem, r_sem in moves:
            dt, dg = mv[0]

            @pl.when(has(-dt, -dg))
            def _(mv=mv, s_sem=s_sem, r_sem=r_sem):
                remote(mv, s_sem, r_sem, -1).wait_recv()

    up_half = 2 * g < m

    def target(i):
        asc = i + (i >= g).astype(jnp.int32)
        x = m - 1 - i
        desc = x - (x <= g).astype(jnp.int32)
        return jnp.where(up_half, desc, asc)

    def warm_piece(i, p):
        to = target(i)
        return pltpu.make_async_remote_copy(
            warm_in.at[pl.ds(p * PL, PL), :, pl.ds(pl.multiple_of(to * LANES, LANES), LANES)],
            T0.at[pl.ds(1 + g * LG + p * PL, PL), PAD:TOP, :],
            ws_sem,
            wr_sem.at[g],
            device_id=(t, to),
            device_id_type=MESH,
        )

    def warm_recv(src):
        part = T0.at[1 + src * LG : 1 + (src + 1) * LG, PAD:TOP, :]
        return pltpu.make_async_remote_copy(
            part, part, ws_sem, wr_sem.at[src], device_id=(t, g), device_id_type=MESH
        )

    def warm_sent():
        part = temp_st.at[0 : (m - 1) * LG]
        pltpu.make_async_remote_copy(
            part, part, ws_sem, wr_sem.at[0], device_id=(t, g), device_id_type=MESH
        ).wait_send()

    outer = jnp.logical_or(g * LG < Q, (g + 1) * LG > L - Q)
    NP = LG // PL
    COUNT = (m - 1) * NP

    def feed(c):
        far = (m - 2) * NP

        def issue(cond, order, start, num, den):
            at = lambda x: lax.div(x * num, den)
            q = at(c - start)
            for e in range(-(-num // den)):

                @pl.when(
                    jnp.logical_and(
                        jnp.logical_and(cond, c >= start),
                        jnp.logical_and(q + e < at(c - start + 1), q + e < COUNT),
                    )
                )
                def _(e=e):
                    warm_piece(*order(q + e)).start()

        def far_first(q):
            near = q >= far
            return (
                jnp.where(near, m - 2, lax.rem(q, m - 2)),
                jnp.where(near, q - far, lax.div(q, m - 2)),
            )

        def in_turn(q):
            return lax.rem(q, m - 1), lax.div(q, m - 1)

        issue(outer, far_first, 0, 1, 1)
        issue(jnp.logical_not(outer), in_turn, 28, 4, 3)

    def warm_arrived(sources):
        for src in sources:

            @pl.when(g == src)
            def _():
                warm_cp.wait()

            @pl.when(g != src)
            def _(src=src):
                warm_recv(src).wait_recv()

    lane = lax.broadcasted_iota(jnp.int32, (SUB, LANES), 1)
    first = lane == 0
    last = lane == LANES - 1
    odd = lax.rem(lane, 2) == 1
    pair = lax.div(lane, 2)
    bottom = lax.broadcasted_iota(jnp.int32, (SUB, LANES), 0) == SUB - 1

    def rows(s, d=0):
        return slice(PAD + s * SUB + d, PAD + s * SUB + d + SUB)

    def tile(s):
        return slice(s * SUB, (s + 1) * SUB)

    HB = L // 2 // (2 * UB)

    def start_of(G, i):
        i = jnp.minimum(i, HB - 1) * (2 * UB)
        if G == I:
            return i + Q, i
        return i + jnp.where(i >= Q, L // 2, 0), i

    def edge_spot(j):
        return (
            lax.rem(2 * LANES - 2 - 2 * j, LANES),
            lax.rem(2 * LANES - 2 - LANES // 2 - 2 * j, LANES),
        )

    def pack_spot(j):
        return (
            (pair == j, 2 * j + 1),
            (pair == j + LANES // 4, lax.rem(2 * j + LANES // 2 + 1, LANES)),
        )

    def pack_vel(k, G, l, j):
        for d in range(UB):
            sp = pack_spot(j + d)
            for s in range(NS):
                for f in range(2):
                    hit, to = sp[f]
                    pltpu.store(
                        pk.at[k, G, rows(s), :],
                        roll(U[k % 2][f, l + d, rows(s), :], to),
                        mask=hit,
                    )

    def pack_first(G):
        def body(i, c):
            l, j = start_of(G, i)
            pack_vel(0, G, l, j)
            pack_vel(0, G, l + UB, j + UB)
            return c

        lax.fori_loop(0, HB, body, 0)

    def merge(k, G):
        for s in range(-1, NS + 1):
            w = jnp.where(odd, crx[k, G, 1, rows(s), :], roll(crx[k, G, 0, rows(s), :], 2))
            mg[G, rows(s), :] = w
            if s == -1:
                low = w
        mg[G, rows(NS), :] = jnp.where(bottom, low, w)

    def side_vel(k, G, l, j, dy, sy):
        V = U[k % 2]
        tiles = NS + 1 if k < SWEEPS else NS
        for d in range(UB):
            sp = edge_spot(j + d)
            for s in range(tiles):
                halo = mg[G, rows(s), :]
                for f in range(2):
                    x = V[f, l + d, rows(s), :]
                    if s == NS:
                        x = jnp.where(bottom, V[f, l + d, rows(-1), :], x)
                    edge = roll(halo, sp[f])
                    up = jnp.where(last, edge, roll(x, LANES - 1))
                    down = jnp.where(first, edge, roll(x, 1))
                    diff = up - down
                    dy[f, d, rows(s), :] = diff
                    if s == NS:
                        dy[f, d, rows(-1), :] = diff
                    elif k < SWEEPS:
                        sy[f, d, tile(s), :] = up + down

    def strain(slot, l, d, s, dy):
        l = l + d
        lm = jnp.maximum(l - 1, 0)
        lp = jnp.minimum(l + 1, L - 1)
        V = U[slot]
        e, w, up, lo = [], [], [], []
        for f in range(2):
            e.append(V[f, l, rows(s, 1), :])
            w.append(V[f, l, rows(s, -1), :])
            up.append(V[f, lp, rows(s), :])
            lo.append(V[f, lm, rows(s), :])
        xu, xv = e[0] - w[0], e[1] - w[1]
        yv = dy[1, d, rows(s), :]
        shear = dy[0, d, rows(s), :] + xv
        du, dv = up[0] - lo[0], up[1] - lo[1]
        total = (xu * (xu + yv) + yv * yv) + 0.25 * (
            (shear * shear + du * du) + dv * dv
        )
        visc = rate[l, tile(s), :] * jnp.exp2(lax.log2(total + 0.04) * (-1.0 / 3.0))
        return e, w, up, lo, total, visc

    def new_vel(k, l, dy, sy):
        slot, new_slot = k % 2, (k + 1) % 2
        for d in range(UB):
            low = jnp.minimum(l + d, 1)
            for s in range(NS):
                e, w, up, lo, _, visc = strain(slot, l, d, s, dy)
                cross_u = dy[1, d, rows(s, 1), :] - dy[1, d, rows(s, -1), :]
                cross_v = dy[0, d, rows(s, 1), :] - dy[0, d, rows(s, -1), :]
                near_u = (
                    4.0 * ((e[0] + w[0]) + (up[0] + lo[0]))
                    + sy[0, d, tile(s), :]
                    + 0.75 * cross_u
                )
                near_v = (
                    4.0 * (sy[1, d, tile(s), :] + (up[1] + lo[1]))
                    + (e[1] + w[1])
                    + 0.75 * cross_v
                )
                scale = 1.0 / (22.0 * visc + cb[2 + low, tile(s), :])
                U[new_slot][0, l + d, rows(s), :] = (cb[0, tile(s), :] + visc * near_u) * scale
                U[new_slot][1, l + d, rows(s), :] = (cb[1, tile(s), :] + visc * near_v) * scale

    def new_heat(l, dy):
        slot = SWEEPS % 2
        for d in range(UB):
            for s in range(NS):
                *_, total, visc = strain(slot, l, d, s, dy)
                q = (0.025 * FOLD) * (visc * total)
                u = 0.05 * U[slot][0, l + d, rows(s), :]
                v = 0.05 * U[slot][1, l + d, rows(s), :]
                west = 0.1 + jnp.maximum(u, 0.0)
                east = 0.1 - jnp.minimum(u, 0.0)
                south = 0.1 + jnp.maximum(v, 0.0)
                north = 0.1 - jnp.minimum(v, 0.0)
                mid = 0.6 - ((west + east) + (south + north))
                for i, x in enumerate((q, west, east, south, north, mid)):
                    coef[i, l + d, tile(s), :] = x

    def sweep(k, G):
        def side(l, j, dy, sy):
            side_vel(k, G, l, j, dy, sy)

        def new(l, dy, sy):
            if k < SWEEPS:
                new_vel(k, l, dy, sy)
            else:
                new_heat(l, dy)

        def pack(l, j):
            if k < SWEEPS:
                pack_vel(k + 1, G, l, j)

        side(*start_of(G, 0), dya, sya)

        def body(i, c):
            l, j = start_of(G, i)
            lb, jb = start_of(G, jnp.maximum(i - 1, 0))
            ln, jn = start_of(G, i + 1)
            if k < SWEEPS:
                feed((2 * k + G) * HB + i)
            pack(lb + UB, jb + UB)
            new(l, dya, sya)
            side(l + UB, j + UB, dyb, syb)
            pack(l, j)
            new(l + UB, dyb, syb)
            side(ln, jn, dya, sya)
            return c

        lax.fori_loop(0, HB, body, 0)
        l, j = start_of(G, HB - 1)
        pack(l + UB, j + UB)

    def pack_th(k, G, l):
        for d in range(UT):
            hit = pair == l + d
            for s in range(NS):
                pltpu.store(
                    tpk.at[k, G, tile(s), :],
                    roll(T[k % 2][l + d + 1, rows(s), :], 2 * (l + d) + 1),
                    mask=hit,
                )

    def blocks(segs):
        counts = [-(-(b - a) // UT) for a, b in segs]
        total = sum(counts) + sum(counts) % 2

        def start(i):
            i = jnp.minimum(i, sum(counts) - 1)
            if len(segs) == 1:
                (a, b), = segs
                return jnp.minimum(a + i * UT, b - UT)
            (a, b), (c, e) = segs
            return jnp.where(
                i < counts[0],
                jnp.minimum(a + i * UT, b - UT),
                jnp.minimum(c + (i - counts[0]) * UT, e - UT),
            )

        return total, start

    def theta_first(G):
        total, start = blocks(th_segs(0, G))

        def body(i, c):
            pack_th(0, G, start(i))
            return c

        lax.fori_loop(0, total, body, 0)

    def th_merge(k, G):
        for s in range(NS):
            w = jnp.where(odd, trx[k, G, 1, tile(s), :], roll(trx[k, G, 0, tile(s), :], 2))
            if G == I:
                (a, b), = th_segs(k, I)
                mine = jnp.logical_and(lane > 2 * a, lane <= 2 * b)
                w = jnp.where(mine, w, tmg[k, tile(s), :])
            tmg[k, tile(s), :] = w

    def side_th(k, l, ns):
        for d in range(UT):
            to = LANES - 2 - 2 * (l + d)
            for s in range(NS):
                x = T[k % 2][l + d + 1, rows(s), :]
                edge = roll(tmg[k, tile(s), :], to)
                ns[0, d, tile(s), :] = jnp.where(last, edge, roll(x, LANES - 1))
                ns[1, d, tile(s), :] = jnp.where(first, edge, roll(x, 1))

    def new_th(k, l, ns):
        V = T[k % 2]
        for d in range(UT):
            x = l + d
            for s in range(NS):
                q, west, east, south, north, mid = [coef[i, x, tile(s), :] for i in range(6)]
                value = (
                    (mid * V[x + 1, rows(s), :] + 0.2 * (V[x + 2, rows(s), :] + V[x, rows(s), :]))
                    + (west * V[x + 1, rows(s, -1), :] + east * V[x + 1, rows(s, 1), :])
                    + ((south * ns[1, d, tile(s), :] + north * ns[0, d, tile(s), :]) + q)
                )
                if k < SECTIONS - 1:
                    T[(k + 1) % 2][x + 1, rows(s), :] = value
                else:
                    temp_st[x, tile(s), :] = value
                    hard_st[x, tile(s), :] = jnp.exp(-0.6 * value)

    def section(k, G):
        total, start = blocks(th_segs(k + 1, G))

        def pack(l):
            if k < SECTIONS - 1:
                pack_th(k + 1, G, l)

        side_th(k, start(0), nsa)

        def body(i, c):
            l, lm, ln = start(2 * i), start(2 * i + 1), start(2 * i + 2)
            pack(start(jnp.maximum(2 * i - 1, 0)))
            new_th(k, l, nsa)
            side_th(k, lm, nsb)
            pack(l)
            new_th(k, lm, nsb)
            side_th(k, ln, nsa)
            return c

        lax.fori_loop(0, total // 2, body, 0)
        pack(start(total - 1))

    def temp_move(i):
        q, a, b = segs_out[i][1:]
        src = temp_st.at[a:b]
        dst = temp_out.at[
            a - q * LG : b - q * LG, :, pl.ds(pl.multiple_of(g * LANES, LANES), LANES)
        ]
        far = pltpu.make_async_remote_copy(
            src, dst, os_sem.at[i], or_sem.at[i, g], device_id=(t, q), device_id_type=MESH
        )
        return far, pltpu.make_async_copy(src, dst, os_sem.at[i])

    def temp_send(i):
        q = segs_out[i][1]

        @pl.when(g != q)
        def _():
            temp_move(i)[0].start()

        @pl.when(g == q)
        def _():
            temp_move(i)[1].start()

    def temp_wait(i):
        q, a, b = segs_out[i][1:]

        @pl.when(g != q)
        def _():
            temp_move(i)[0].wait_send()

        @pl.when(g == q)
        def _():
            temp_move(i)[1].wait()
            for src in range(m):
                if src != q:
                    dst = temp_out.at[
                        a - q * LG : b - q * LG, :, src * LANES : (src + 1) * LANES
                    ]
                    pltpu.make_async_remote_copy(
                        dst, dst, os_sem.at[i], or_sem.at[i, src],
                        device_id=(t, g), device_id_type=MESH,
                    ).wait_recv()

    for G in (O, I):
        send(vel_moves(0, G, "row"))
    for G in (O, I):
        for cp in vel_cp[G]:
            cp.wait()
        pack_first(G)
        send(vel_moves(0, G, "col"))
    ice = icy[...].astype(f32)
    water = (1.0 - ice) * (1.0 / FOLD)
    cb[0] = ice * grav[0] * (1.0 / FOLD)
    cb[1] = ice * grav[1] * (1.0 / FOLD)
    cb[2] = water + slide[...] * bed[...].astype(f32) * (1.0 / FOLD)
    cb[3] = water
    cb[4] = ice
    rate_cp.wait()

    def ice_rate(i, c):
        for d in range(UT):
            for s in range(NS):
                rate[i * UT + d, tile(s), :] = rate[i * UT + d, tile(s), :] * cb[4, tile(s), :]
        return c

    lax.fori_loop(0, L // UT, ice_rate, 0)

    vel_back = {
        G: [
            pltpu.make_async_copy(
                U[SWEEPS % 2].at[:, a:b, PAD:TOP, :], vel_out.at[:, a:b], hs_sem.at[2 * G + i]
            )
            for i, (a, b) in enumerate(SEGS[G])
        ]
        for G in (O, I)
    }
    def owners(G):
        return sorted({q for q in range(m) for a, b in th_segs(0, G) if a < (q + 1) * LG and b > q * LG})

    def heat_part(G):
        received(vel_moves(SWEEPS, G, "all"))
        merge(SWEEPS, G)
        sweep(SWEEPS, G)

    def th_part(k, G):
        received(th_moves(k, G))
        th_merge(k, G)
        if k:
            sent(th_moves(k - 1, G))
        section(k, G)
        if k < SECTIONS - 1:
            send(th_moves(k + 1, G))
        else:
            for cp in hard_back[G]:
                cp.start()

    def th_start(G, known=()):
        warm_arrived([q for q in owners(G) if q not in known])
        theta_first(G)
        send(th_moves(0, G))

    hard_back = {
        G: [
            pltpu.make_async_copy(hard_st.at[a:b], hard_out.at[a:b], hs_sem.at[4 + 2 * G + i])
            for i, (a, b) in enumerate(th_segs(SECTIONS, G))
        ]
        for G in (O, I)
    }

    def temp_out_part(G):
        for i, sg in enumerate(segs_out):
            if sg[0] == G:
                temp_send(i)

    for k in range(SWEEPS):
        for G in (O, I):
            received(vel_moves(k, G, "all"))
            if k:
                sent(vel_moves(k - 1, G, "all"))
            merge(k, G)
            sweep(k, G)
            send(vel_moves(k + 1, G, "all"))
            if k == SWEEPS - 1:
                for cp in vel_back[G]:
                    cp.start()
                if G == O:
                    th_start(O)

    heat_part(O)
    th_part(0, O)
    th_start(I, owners(O))
    heat_part(I)
    th_part(1, O)
    th_part(0, I)
    th_part(2, O)
    th_part(1, I)
    th_part(3, O)
    th_part(2, I)
    temp_out_part(O)
    th_part(3, I)
    temp_out_part(I)

    for i in range(len(segs_out)):
        temp_wait(i)
    warm_sent()
    for G in (O, I):
        for cp in vel_back[G] + hard_back[G]:
            cp.wait()
        sent(vel_moves(SWEEPS - 1, G, "all"))
        sent(vel_moves(SWEEPS, G, "all"))
        sent(th_moves(SECTIONS - 1, G))


def hand_over_kernel(a, b, c, x, y, z, va, vb, vc, in_sem, out_sem):
    parts = []
    for src, mid, dst in ((a, va, x), (c, vc, z), (b, vb, y)):
        pieces = src.shape[0] if len(src.shape) == 4 else 1
        for i in range(pieces):
            for j in range(PARTS):
                at = (i,) if len(src.shape) == 4 else ()
                size = src.shape[len(at)] // PARTS
                at += (slice(j * size, (j + 1) * size),)
                parts.append((src.at[at], mid.at[at], dst.at[at]))
    ins = [pltpu.make_async_copy(s, v, in_sem.at[i]) for i, (s, v, _) in enumerate(parts)]
    outs = [pltpu.make_async_copy(v, d, out_sem.at[i]) for i, (_, v, d) in enumerate(parts)]
    for cp in ins:
        cp.start()
    for cp, back in zip(ins, outs):
        cp.wait()
        back.start()
    for back in outs:
        back.wait()


def hand_over(arrays):
    any_spec = pl.BlockSpec(memory_space=pl.ANY)
    count = PARTS * sum(x.shape[0] if x.ndim == 4 else 1 for x in arrays)
    return pl.pallas_call(
        hand_over_kernel,
        out_shape=tuple(jax.ShapeDtypeStruct(x.shape, x.dtype) for x in arrays),
        in_specs=[any_spec] * 3,
        out_specs=(any_spec,) * 3,
        scratch_shapes=[pltpu.VMEM(x.shape, x.dtype) for x in arrays]
        + [pltpu.SemaphoreType.DMA((count,))] * 2,
        compiler_params=pltpu.CompilerParams(vmem_limit_bytes=60 * 1024 * 1024),
        name="hand_over",
    )(*arrays)


def local(n, m, vel, rate, warm, grav, slide, icy, bed):
    _, L, R, Y = vel.shape
    LG = L // m
    assert Y == LANES and R % SUB == 0 and L % (16 * UB) == 0 and LG % PL == 0 and m > 2
    assert 2 * L == LANES and L // 4 >= SECTIONS + UT
    f32 = jnp.float32
    Q = L // 4
    cut = SECTIONS
    parts = [(0, 0, Q - cut), (0, L - Q + cut, L), (1, Q - cut, L - Q + cut)]
    segs_out = []
    for G, a, b in parts:
        while a < b:
            q = a // LG
            e = min(b, (q + 1) * LG)
            segs_out.append((G, q, a, e))
            a = e
    segs_out = tuple(segs_out)
    any_spec = pl.BlockSpec(memory_space=pl.ANY)
    vmem = pl.BlockSpec(memory_space=pltpu.VMEM)
    K = SWEEPS + 1
    H = R + 2 * PAD
    V = pltpu.VMEM
    dma = pltpu.SemaphoreType.DMA
    out = pl.pallas_call(
        functools.partial(kernel, n, m, R, L, LG, segs_out),
        out_shape=(
            jax.ShapeDtypeStruct(vel.shape, f32),
            jax.ShapeDtypeStruct(warm.shape, f32),
            jax.ShapeDtypeStruct(rate.shape, f32),
        ),
        in_specs=[any_spec] * 3 + [vmem] * 4,
        out_specs=(any_spec,) * 3,
        scratch_shapes=[
            V((2, L, H, LANES), f32),
            V((2, L, H, LANES), f32),
            V((L + 2, H, LANES), f32),
            V((L + 2, H, LANES), f32),
            V((L, R, LANES), f32),
            V((6, L, R, LANES), f32),
            V((L, R, LANES), f32),
            V((L, R, LANES), f32),
            V((5, R, LANES), f32),
            V((2, UB, H, LANES), f32),
            V((2, UB, H, LANES), f32),
            V((2, UB, R, LANES), f32),
            V((2, UB, R, LANES), f32),
            V((2, UT, R, LANES), f32),
            V((2, UT, R, LANES), f32),
            V((K, 2, H, LANES), f32),
            V((K, 2, 2, H, LANES), f32),
            V((2, H, LANES), f32),
            V((SECTIONS, 2, R, LANES), f32),
            V((SECTIONS, 2, 2, R, LANES), f32),
            V((SECTIONS, R, LANES), f32),
            dma((6,)),
            dma((K, 2, 10)),
            dma((K, 2, 10)),
            dma((SECTIONS, 2, 6)),
            dma((SECTIONS, 2, 6)),
            dma,
            dma((m,)),
            dma((len(segs_out),)),
            dma((len(segs_out), m)),
            dma((8,)),
        ],
        compiler_params=pltpu.CompilerParams(
            collective_id=0, has_side_effects=True, vmem_limit_bytes=60 * 1024 * 1024
        ),
        name="ice_step",
    )(vel, rate, warm, grav, slide, icy, bed)
    return hand_over(out)


def solution(mesh):
    return jax.shard_map(
        functools.partial(local, mesh.shape["tile"], mesh.shape["grp"]),
        mesh=mesh,
        in_specs=(
            P(None, None, "tile", "grp"),
            P(None, "tile", "grp"),
            P("grp", "tile", None),
            P(None, "tile", "grp"),
            P("tile", "grp"),
            P("tile", "grp"),
            P("tile", "grp"),
        ),
        out_specs=(P(None, None, "tile", "grp"), P("grp", "tile", None), P(None, "tile", "grp")),
        check_vma=False,
    )
```
